32 devices in a mesh: row: 8 (over z, core), col: 4 (over y, x).
Axes of the slice: x: 2, y: 2, z: 4, core: 2. Of those that a mesh axis runs over, the one named last changes fastest.
Arguments:
- features: bfloat16 [8192, 256], P(('row', 'col')), may hold values from -6 to 6
- weight_in: bfloat16 [2, 256, 256], replicated, may hold values from -0.21875 to 0.21875
- weight_out: bfloat16 [2, 256, 256], replicated, may hold values from -0.21875 to 0.21875
- weight_self: bfloat16 [2, 256, 256], replicated, may hold values from -0.21875 to 0.21875
- layer_bias: float32 [2, 256], replicated, may hold values from -3 to 3
- out_degree: int32 [8192], P(('row', 'col')), may hold values from 1 to 64
- in_degree: int32 [8192], P(('row', 'col')), may hold values from 1 to 64
- tile_values: bfloat16 [4096, 128, 128], P(('row', 'col')), may hold values from 0 to 1
- tile_pick: int32 [4096], P(('row', 'col')), may hold values from 0 to 3
- tile_count: int32 [32], P(('row', 'col')), may hold values from 1 to 128, as said below
- cotangent: bfloat16 [8192, 256], P(('row', 'col')), may hold values from -6 to 6
Outputs:
- out_features: bfloat16 [8192, 256], P(('row', 'col'))
- grad_features: float32 [8192, 256], P(('row', 'col'))
- grad_weight_in: float32 [2, 256, 256], replicated
- grad_weight_out: float32 [2, 256, 256], replicated
- grad_weight_self: float32 [2, 256, 256], replicated
- grad_bias: float32 [2, 256], replicated
The draws below stay inside these ranges and needn't reach their ends.
Inputs may be any that keep to these rules, and one draw needn't show every extreme that they name: `tile_count`: slots at or above a device's count are empty and unused; in every draw some device has all 128 slots live. `tile_pick`: slot s of a device belongs to group s // (128 // 32), which fixes the node square of its tile as in the definition of A.
All inputs are finite; a program needn't handle non-finite values.
Results may differ from the reference program's by a relative error of at most 0.025.
Values may be sent and summed in bfloat16 or wider, within the bound.
A program may use at most 128 MiB of HBM per device.

```python
import jax
import jax.numpy as jnp
from jax import lax

F = 256
TILE = 128
TILES = 128
LAYERS = 2
NODES = 8192
BLK = 2
N_COL = 4
DEVICES = 32


def draw_tile_count(key, part):
    first_key, second_key = jax.random.split(jax.random.fold_in(key, 17))
    uniform_ints = jax.random.randint(first_key, (DEVICES,), 0, TILES, dtype=jnp.int32)
    counts = 1 + uniform_ints * uniform_ints // TILES
    fullest = jax.random.randint(second_key, (), 0, DEVICES, dtype=jnp.int32)
    device_ids = jnp.arange(DEVICES, dtype=jnp.int32)
    return jnp.where(device_ids == fullest, TILES, counts).astype(jnp.int32)


def plant(entries, rng, least, high):
    longest = entries.shape.index(max(entries.shape))
    spots = []
    for shift in (0, 1):
        where = [jax.random.randint(jax.random.fold_in(rng, axis), (), 0, length) for axis, length in enumerate(entries.shape)]
        where[longest] = (where[longest] + shift) % entries.shape[longest]
        spots.append(tuple(where))
    return entries.at[spots[0]].set(least).at[spots[1]].set(high)


def shard_levels(key, dims, cuts, least, high):
    factor_of = 1.0
    for position, shards_of in cuts:
        heights = jax.random.uniform(jax.random.fold_in(jax.random.fold_in(key, 6), position), (shards_of,), jnp.float32, least / len(cuts), high / len(cuts))
        factor_of = factor_of * jnp.repeat(jnp.exp(heights), dims[position] // shards_of).reshape((-1,) + (1,) * (len(dims) - 1 - position))
    return factor_of


def centred(key, dims, deviation, reach, cuts=(), kind=jnp.bfloat16):
    factor_of = shard_levels(key, dims, cuts, -0.22, 0.18) if cuts else 1.0
    array = jax.random.normal(key, dims, jnp.float32) * deviation * factor_of
    return jnp.minimum(jnp.maximum(array, -reach), reach).astype(kind)


def setup_inputs(seed: int = 0) -> dict:
    splits = jax.random.split(jax.random.key(seed), 12)
    features = centred(splits[0], (NODES, F), 1.0, 6.0, ((0, 32),))
    weight_in = centred(splits[1], (LAYERS, F, F), (3 * F) ** -0.5, 0.21875)
    weight_out = centred(splits[2], (LAYERS, F, F), (3 * F) ** -0.5, 0.21875)
    weight_self = centred(splits[3], (LAYERS, F, F), (3 * F) ** -0.5, 0.21875)
    layer_bias = centred(splits[4], (LAYERS, F), 0.5, 3.0, (), jnp.float32)
    out_degree = plant(jax.random.randint(splits[5], (NODES,), 1, 65), jax.random.fold_in(splits[5], 1), 1, 64).astype(jnp.int32)
    in_degree = plant(jax.random.randint(splits[6], (NODES,), 1, 65), jax.random.fold_in(splits[6], 1), 1, 64).astype(jnp.int32)
    tile_values = jnp.clip(1.0 * jax.random.uniform(splits[7], (DEVICES * TILES, TILE, TILE), jnp.float32) ** shard_levels(splits[7], (DEVICES * TILES, TILE, TILE), ((0, 32),), -0.2, 0.2), 0.0, 1.0).astype(jnp.bfloat16)
    tile_pick = plant(jax.random.randint(splits[8], (DEVICES * TILES,), 0, BLK * BLK), jax.random.fold_in(splits[8], 1), 0, (BLK * BLK) - 1).astype(jnp.int32)
    tile_count = draw_tile_count(jax.random.fold_in(splits[11], 71), 0)
    cotangent = centred(splits[10], (NODES, F), 1.0, 6.0, ((0, 32),))
    return {"features": features, "weight_in": weight_in, "weight_out": weight_out, "weight_self": weight_self, "layer_bias": layer_bias, "out_degree": out_degree, "in_degree": in_degree, "tile_values": tile_values, "tile_pick": tile_pick, "tile_count": tile_count, "cotangent": cotangent}


def activation(inputs):
    return jax.nn.gelu(inputs, approximate=True)

def sparse_product(operand, tile_values, tile_pick, tile_count, transposed):
    node_blocks = operand.reshape(NODES // TILE, TILE, F)
    per_peer = TILES // DEVICES
    slot_ids = jnp.arange(TILES, dtype=jnp.int32)
    dest_group = slot_ids // per_peer

    def add_device(running, device_id):
        tile_vals = lax.dynamic_slice_in_dim(tile_values, device_id * TILES, TILES, 0).astype(jnp.float32)
        tile_picks = lax.dynamic_slice_in_dim(tile_pick, device_id * TILES, TILES, 0)
        row_id = device_id // N_COL
        col_id = device_id % N_COL
        row_blocks = ((row_id * N_COL + dest_group % N_COL) * BLK + tile_picks // BLK).astype(jnp.int32)
        col_blocks = ((dest_group // N_COL * N_COL + col_id) * BLK + tile_picks % BLK).astype(jnp.int32)
        live_mask = slot_ids < tile_count[device_id]
        if transposed:
            from_blocks, to_blocks, einsum_form = (row_blocks, col_blocks, 'sji,sjf->sif')
        else:
            from_blocks, to_blocks, einsum_form = (col_blocks, row_blocks, 'sij,sjf->sif')
        gathered = jnp.take(node_blocks, from_blocks, axis=0).astype(jnp.float32)
        product = jnp.einsum(einsum_form, tile_vals, gathered, precision=lax.Precision.HIGHEST)
        product = jnp.where(live_mask[:, None, None], product, jnp.zeros_like(product))
        return (running.at[to_blocks].add(product), None)
    start_value = jnp.zeros((NODES // TILE, TILE, F), jnp.float32)
    running, unused = lax.scan(add_device, start_value, jnp.arange(DEVICES, dtype=jnp.int32))
    return running.reshape(NODES, F)

def reference(features, weight_in, weight_out, weight_self, layer_bias, out_degree, in_degree, tile_values, tile_pick, tile_count, cotangent):
    scale_in = (1.0 / jnp.sqrt(in_degree.astype(jnp.float32)))[:, None]
    scale_out = (1.0 / jnp.sqrt(out_degree.astype(jnp.float32)))[:, None]
    hidden = features
    stored = []
    for layer in range(LAYERS):
        scaled_in = (scale_in * hidden.astype(jnp.float32)).astype(jnp.bfloat16)
        scaled_out = (scale_out * hidden.astype(jnp.float32)).astype(jnp.bfloat16)
        msg_in = (scale_out * sparse_product(scaled_in, tile_values, tile_pick, tile_count, False)).astype(jnp.bfloat16)
        msg_out = (scale_in * sparse_product(scaled_out, tile_values, tile_pick, tile_count, True)).astype(jnp.bfloat16)
        preact = jnp.dot(msg_in, weight_in[layer], preferred_element_type=jnp.float32)
        preact = preact + jnp.dot(msg_out, weight_out[layer], preferred_element_type=jnp.float32)
        preact = preact + jnp.dot(hidden, weight_self[layer], preferred_element_type=jnp.float32)
        preact = preact + layer_bias[layer].astype(jnp.float32)[None, :]
        stored.append((hidden, msg_in, msg_out, preact))
        hidden = activation(preact).astype(jnp.bfloat16)
    out_features = hidden
    upstream = cotangent.astype(jnp.float32)
    grads_in, grads_out, grads_self, grads_bias = ([], [], [], [])
    for layer in reversed(range(LAYERS)):
        hidden, msg_in, msg_out, preact = stored[layer]
        unused, pullback = jax.vjp(activation, preact)
        grad_z = pullback(upstream)[0].astype(jnp.bfloat16)
        grads_in.append(jnp.dot(msg_in.T, grad_z, preferred_element_type=jnp.float32))
        grads_out.append(jnp.dot(msg_out.T, grad_z, preferred_element_type=jnp.float32))
        grads_self.append(jnp.dot(hidden.T, grad_z, preferred_element_type=jnp.float32))
        grads_bias.append(lax.optimization_barrier(jnp.sum(grad_z.astype(jnp.float32), axis=0)))
        back_in = (scale_out * jnp.dot(grad_z, weight_in[layer].T, preferred_element_type=jnp.float32)).astype(jnp.bfloat16)
        back_out = (scale_in * jnp.dot(grad_z, weight_out[layer].T, preferred_element_type=jnp.float32)).astype(jnp.bfloat16)
        upstream = scale_in * sparse_product(back_in, tile_values, tile_pick, tile_count, True)
        upstream = upstream + scale_out * sparse_product(back_out, tile_values, tile_pick, tile_count, False)
        upstream = upstream + jnp.dot(grad_z, weight_self[layer].T, preferred_element_type=jnp.float32)
    return (out_features, upstream, jnp.stack(grads_in[::-1]), jnp.stack(grads_out[::-1]), jnp.stack(grads_self[::-1]), jnp.stack(grads_bias[::-1]))
```

```python
import functools

import jax
import jax.numpy as jnp
from jax import lax
from jax.experimental import pallas as pl
from jax.experimental.pallas import tpu as pltpu
from jax.sharding import PartitionSpec as P

MESH = pl.DeviceIdType.MESH
F32 = jnp.float32
BF16 = jnp.bfloat16
EXTRA = 16
C0 = 0.7978845608028654
C1 = 0.044715


def gelu(v):
    return 0.5 * v * (1.0 + jnp.tanh(C0 * (v + C1 * (v * v * v))))


def gelu_slope(v):
    t = jnp.tanh(C0 * (v + C1 * (v * v * v)))
    return 0.5 * (1.0 + t) + 0.5 * v * (1.0 - t * t) * (C0 * (1.0 + 3.0 * C1 * (v * v)))


def dot(a, b):
    return jnp.dot(a, b, preferred_element_type=F32)


def dot_nt(a, b):
    return lax.dot_general(a, b, (((1,), (1,)), ((), ())), preferred_element_type=F32)


def dot_tn(a, b):
    return lax.dot_general(a, b, (((0,), (0,)), ((), ())), preferred_element_type=F32)


def kernel(
    rows,
    cols,
    feat,
    w_in,
    w_out,
    w_self,
    bias,
    out_deg,
    in_deg,
    cot,
    pick,
    count,
    tiles,
    out_ref,
    gfeat_ref,
    parts_ref,
    block,
    sib_block,
    staged,
    xc,
    xr,
    send_d,
    recv_d,
    send_r,
    recv_r,
    own_d,
    own_r,
    s_in,
    s_out,
    hs,
    ms_in,
    ms_out,
    zs,
    up,
    gz_ref,
    tile_sem,
    blk_sem,
    xr_sem,
    xrs_sem,
    xcr_sem,
    xcl_sem,
    xcs_sem,
    d_sem,
    r_sem,
):
    chips = rows // 2
    nodes, width = feat.shape
    layers = w_in.shape[0]
    tile = staged.shape[1]
    sub = nodes // tile
    slots = staged.shape[0]
    per = slots // (rows * cols)
    row = lax.axis_index("row")
    c = lax.axis_index("col")
    k = lax.rem(row, 2)
    z = row // 2
    other = 1 - k
    sibling = (2 * z + other, c)

    def remote(src, dst, sems, index, device, parity=None):
        where = (index,) if parity is None else (parity, index)
        return pltpu.make_async_remote_copy(
            src_ref=src,
            dst_ref=dst,
            send_sem=sems.at[(0,) + where],
            recv_sem=sems.at[(1,) + where],
            device_id=device,
            device_id_type=MESH,
        )

    def at_chip(zz):
        return (2 * zz + k, c)

    def at_col(cc):
        return (row, cc)

    barrier = pltpu.get_barrier_semaphore()
    pl.semaphore_signal(barrier, inc=1, device_id=sibling, device_id_type=MESH)
    for off in range(1, chips):
        pl.semaphore_signal(
            barrier, inc=1, device_id=at_chip(lax.rem(z + off, chips)), device_id_type=MESH
        )
    for off in range(1, cols):
        pl.semaphore_signal(
            barrier, inc=1, device_id=at_col(lax.rem(c + off, cols)), device_id_type=MESH
        )

    strip = cols * per

    def tile_copy(rr):
        span = pl.ds(rr * strip, strip)
        return pltpu.make_async_copy(tiles.at[span], staged.at[span], tile_sem.at[rr])

    for kk in (other, k):
        for zz in range(chips):
            tile_copy(2 * zz + kk).start()

    for deg, scale in ((out_deg, s_out), (in_deg, s_in)):
        line = 1.0 / jnp.sqrt(deg[...].astype(F32))
        scale[...] = jnp.transpose(jnp.broadcast_to(line, (width, nodes)))
    hs[0] = feat[...]

    pl.semaphore_wait(barrier, chips + cols - 1)

    def build():
        for kk in (other, k):

            @pl.loop(0, chips)
            def _(zz):
                rr = 2 * zz + kk
                tile_copy(rr).wait()

                @pl.loop(0, cols)
                def _(cc):
                    first = (rr * cols + cc) * per
                    values = []
                    weights = []
                    for s in range(per):
                        values.append(staged[first + s].astype(F32))
                        live = first + s < count[0]
                        weights.append(jnp.where(live, pick[first + s], -1))
                    for spot in range(sub * sub):
                        total = jnp.zeros((tile, tile), F32)
                        for s in range(per):
                            factor = jnp.where(weights[s] == spot, 1.0, 0.0)
                            total = total + factor * values[s]
                        top = pl.multiple_of(cc * nodes + (spot // sub) * tile, tile)
                        left = pl.multiple_of(zz * nodes + (spot % sub) * tile, tile)
                        block[kk, pl.ds(top, tile), pl.ds(left, tile)] = total.astype(BF16)

            if kk is other:
                remote(block.at[other], sib_block, blk_sem, 0, sibling).start()

    def window(zz):
        return pl.ds(pl.multiple_of(zz * nodes, nodes), nodes)

    def exchange(stage, first, second_t):
        p = lax.rem(stage, 2)

        def xr_copy(off):
            mine = xr.at[p, k, :, window(c)]
            return remote(mine, mine, xr_sem, off, at_col(lax.rem(c + off, cols)), p)

        def xrs_copy(off, kk):
            view = xr.at[p, kk, :, window(lax.rem(c + cols - off, cols))]
            return remote(view, view, xrs_sem, off, sibling, p)

        def xc_view(kk, zz):
            return xc.at[p, kk, window(zz), :]

        def xcr_copy(dist, zz):
            return remote(xc_view(k, zz), xc_view(k, zz), xcr_sem, dist, at_chip(z + 1), p)

        def xcl_copy(dist, zz):
            return remote(xc_view(k, zz), xc_view(k, zz), xcl_sem, dist, at_chip(z - 1), p)

        def xcs_copy(kk, zz):
            return remote(xc_view(kk, zz), xc_view(kk, zz), xcs_sem, zz, sibling, p)

        def d_copy(off):
            target = at_col(lax.rem(c + off, cols))
            return remote(send_d.at[off], recv_d.at[p, off], d_sem, off, target, p)

        def r_copy(off):
            target = at_chip(lax.rem(z + off, chips))
            return remote(send_r.at[off], recv_r.at[p, off], r_sem, off, target, p)

        xr[p, k, :, window(c)] = second_t
        xc[p, k, window(z), :] = first
        for off in range(1, cols):
            xr_copy(off).start()
        xrs_copy(0, k).start()

        @pl.when(z + 1 < chips)
        def _():
            xcr_copy(1, z).start()

        @pl.when(z > 0)
        def _():
            xcl_copy(1, z).start()

        xcs_copy(k, z).start()

        @pl.when(stage == 0)
        def _():
            build()

        def take_xr(off):
            source = lax.rem(c + cols - off, cols)
            view = xr.at[p, k, :, window(source)]
            remote(view, view, xr_sem, off, at_col(source), p).wait_recv()
            xrs_copy(off, k).start()

        def take_xc(dist):
            @pl.when(z - dist >= 0)
            def _():
                xcr_copy(dist, z - dist).wait_recv()

                @pl.when(z + 1 < chips)
                def _():
                    xcr_copy(dist + 1, z - dist).start()

                xcs_copy(k, z - dist).start()

            @pl.when(z + dist < chips)
            def _():
                xcl_copy(dist, z + dist).wait_recv()

                @pl.when(z > 0)
                def _():
                    xcl_copy(dist + 1, z + dist).start()

                xcs_copy(k, z + dist).start()

        for off in range(1, cols):
            take_xr(off)
            if off == 1:
                take_xc(1)
        for off in range(cols):
            xrs_copy(off, other).wait_recv()

        @pl.when(stage == 0)
        def _():
            remote(block.at[other], sib_block, blk_sem, 0, sibling).wait_recv()

        lanes = lax.broadcasted_iota(jnp.int32, (EXTRA, nodes), 1)
        groups = lax.broadcasted_iota(jnp.int32, (EXTRA, nodes), 0) // (EXTRA // sub)
        chooser = jnp.where(lanes == groups * tile, 1.0, 0.0).astype(BF16)

        @pl.loop(0, chips)
        def _(step):
            off = lax.rem(step + 1, chips)
            at = window(lax.rem(z + off, chips))
            piece = dot(xr[p, k], block[k, :, at]) + dot(xr[p, other], sib_block[:, at])

            @pl.when(off > 0)
            def _():
                means = []
                for part in range(sub):
                    mean = jnp.mean(piece[:, part * tile : (part + 1) * tile], axis=1, keepdims=True)
                    means.append(jnp.broadcast_to(mean, (width, tile)))
                mean = jnp.concatenate(means, axis=1).astype(BF16)
                send_r[off, pl.ds(0, width), :] = (piece - mean.astype(F32)).astype(BF16)
                send_r[off, pl.ds(width, EXTRA), :] = dot_nt(chooser, mean).astype(BF16)
                r_copy(off).start()

            @pl.when(off == 0)
            def _():
                own_r[...] = piece

        for dist in range(2, chips):
            take_xc(dist)

        @pl.loop(0, chips)
        def _(zz):
            xcs_copy(other, zz).wait_recv()

        @pl.loop(0, cols)
        def _(step):
            off = lax.rem(step + 1, cols)
            at = window(lax.rem(c + off, cols))
            piece = dot(block[0, at, :], xc[p, 0]) + dot(block[1, at, :], xc[p, 1])

            @pl.when(off > 0)
            def _():
                lines = []
                for part in range(sub):
                    span = slice(part * tile, (part + 1) * tile)
                    mean = jnp.mean(piece[span], axis=0, keepdims=True).astype(BF16).astype(F32)
                    send_d[off, pl.ds(part * tile, tile), :] = (piece[span] - mean).astype(BF16)
                    lines.append(jnp.broadcast_to(mean, (EXTRA // sub, width)))
                send_d[off, pl.ds(nodes, EXTRA), :] = jnp.concatenate(lines, axis=0).astype(BF16)
                d_copy(off).start()

            @pl.when(off == 0)
            def _():
                own_d[...] = piece

        def spread(lines):
            reach = EXTRA // sub
            return jnp.concatenate(
                [
                    jnp.broadcast_to(lines[part * reach : part * reach + 1], (tile, width))
                    for part in range(sub)
                ],
                axis=0,
            )

        lines = jnp.zeros((EXTRA, width), F32)
        for off in range(1, cols):
            d_copy(off).wait_recv()
            own_d[...] += recv_d[p, off, pl.ds(0, nodes), :].astype(F32)
            lines = lines + recv_d[p, off, pl.ds(nodes, EXTRA), :].astype(F32)
        direct = own_d[...] + spread(lines)
        lines = jnp.zeros((EXTRA, width), F32)
        for off in range(1, chips):
            r_copy(off).wait_recv()
            own_r[...] += recv_r[p, off, pl.ds(0, width), :].astype(F32)
            lines = lines + recv_r[p, off, pl.ds(width, EXTRA), :].astype(F32)
        reverse = jnp.transpose(own_r[...]) + spread(lines)

        for off in range(1, cols):
            xr_copy(off).wait_send()
            d_copy(off).wait_send()
        for off in range(cols):
            xrs_copy(off, k).wait_send()
        for off in range(1, chips):
            r_copy(off).wait_send()

        @pl.loop(0, chips)
        def _(zz):
            xcs_copy(k, zz).wait_send()

        for dist in range(1, chips):

            @pl.when(jnp.logical_and(z - dist + 1 >= 0, z + 1 < chips))
            def _():
                xcr_copy(dist, z - dist + 1).wait_send()

            @pl.when(jnp.logical_and(z + dist - 1 < chips, z > 0))
            def _():
                xcl_copy(dist, z + dist - 1).wait_send()

        return direct, reverse

    @pl.loop(0, layers)
    def _(layer):
        hidden = hs[layer].astype(F32)
        first = (s_in[...] * hidden).astype(BF16)
        second_t = jnp.transpose(s_out[...] * hidden).astype(BF16)
        direct, reverse = exchange(layer, first, second_t)
        msg_in = (s_out[...] * direct).astype(BF16)
        msg_out = (s_in[...] * reverse).astype(BF16)
        ms_in[layer] = msg_in
        ms_out[layer] = msg_out
        preact = dot(msg_in, w_in[layer]) + dot(msg_out, w_out[layer])
        preact = preact + dot(hs[layer], w_self[layer]) + bias[pl.ds(layer, 1), :]
        zs[layer] = preact
        hs[layer + 1] = gelu(preact).astype(BF16)

    out_ref[...] = hs[layers]
    up[...] = cot[...].astype(F32)

    @pl.loop(0, layers)
    def _(step):
        layer = layers - 1 - step
        grad_z = (up[...] * gelu_slope(zs[layer])).astype(BF16)
        gz_ref[...] = grad_z
        back_in = jnp.transpose(s_out[...] * dot_nt(grad_z, w_in[layer])).astype(BF16)
        back_out = (s_in[...] * dot_nt(grad_z, w_out[layer])).astype(BF16)
        direct, reverse = exchange(layers + step, back_out, back_in)
        up[...] = (
            s_out[...] * direct + s_in[...] * reverse + dot_nt(gz_ref[...], w_self[layer])
        )
        grad_z = gz_ref[...]
        parts_ref[layer, pl.ds(0, width), :] = dot_tn(ms_in[layer], grad_z)
        parts_ref[layer, pl.ds(width, width), :] = dot_tn(ms_out[layer], grad_z)
        parts_ref[layer, pl.ds(2 * width, width), :] = dot_tn(hs[layer], grad_z)
        line = jnp.sum(grad_z.astype(F32), axis=0, keepdims=True)
        tail = parts_ref.shape[1] - 3 * width
        parts_ref[layer, pl.ds(3 * width, tail), :] = jnp.broadcast_to(line, (tail, width))

    gfeat_ref[...] = up[...]
    remote(block.at[other], sib_block, blk_sem, 0, sibling).wait_send()


def per_device(
    features,
    weight_in,
    weight_out,
    weight_self,
    layer_bias,
    out_degree,
    in_degree,
    tile_values,
    tile_pick,
    tile_count,
    cotangent,
):
    rows = lax.axis_size("row")
    cols = lax.axis_size("col")
    nodes, width = features.shape
    layers = weight_in.shape[0]
    slots, tile, unused = tile_values.shape
    chips = rows // 2
    tail = 64
    vmem = pl.BlockSpec(memory_space=pltpu.VMEM)
    smem = pl.BlockSpec(memory_space=pltpu.SMEM)
    sems = pltpu.SemaphoreType.DMA
    out, gfeat, parts = pl.pallas_call(
        functools.partial(kernel, rows, cols),
        out_shape=(
            jax.ShapeDtypeStruct((nodes, width), BF16),
            jax.ShapeDtypeStruct((nodes, width), F32),
            jax.ShapeDtypeStruct((layers, 3 * width + tail, width), F32),
        ),
        in_specs=[vmem] * 8 + [smem] * 2 + [pl.BlockSpec(memory_space=pl.ANY)],
        out_specs=(vmem, vmem, vmem),
        scratch_shapes=[
            pltpu.VMEM((2, cols * nodes, chips * nodes), BF16),
            pltpu.VMEM((cols * nodes, chips * nodes), BF16),
            pltpu.VMEM((slots, tile, tile), BF16),
            pltpu.VMEM((2, 2, chips * nodes, width), BF16),
            pltpu.VMEM((2, 2, width, cols * nodes), BF16),
            pltpu.VMEM((cols, nodes + EXTRA, width), BF16),
            pltpu.VMEM((2, cols, nodes + EXTRA, width), BF16),
            pltpu.VMEM((chips, width + EXTRA, nodes), BF16),
            pltpu.VMEM((2, chips, width + EXTRA, nodes), BF16),
            pltpu.VMEM((nodes, width), F32),
            pltpu.VMEM((width, nodes), F32),
            pltpu.VMEM((nodes, width), F32),
            pltpu.VMEM((nodes, width), F32),
            pltpu.VMEM((layers + 1, nodes, width), BF16),
            pltpu.VMEM((layers, nodes, width), BF16),
            pltpu.VMEM((layers, nodes, width), BF16),
            pltpu.VMEM((layers, nodes, width), F32),
            pltpu.VMEM((nodes, width), F32),
            pltpu.VMEM((nodes, width), BF16),
            sems((rows,)),
            sems((2, 1)),
            sems((2, 2, cols)),
            sems((2, 2, cols)),
            sems((2, 2, chips + 1)),
            sems((2, 2, chips + 1)),
            sems((2, 2, chips)),
            sems((2, 2, cols)),
            sems((2, 2, chips)),
        ],
        compiler_params=pltpu.CompilerParams(
            collective_id=0, has_side_effects=True, vmem_limit_bytes=63 * 1024 * 1024
        ),
    )(
        features,
        weight_in,
        weight_out,
        weight_self,
        layer_bias,
        out_degree.reshape(1, nodes),
        in_degree.reshape(1, nodes),
        cotangent,
        tile_pick,
        tile_count,
        tile_values,
    )
    total = parts.reshape(-1, width)
    total = lax.psum_scatter(total, "row", scatter_dimension=0, tiled=True)
    total = lax.psum_scatter(total, "col", scatter_dimension=0, tiled=True)
    total = lax.all_gather(total, ("row", "col"), axis=0, tiled=True)
    total = total.reshape(layers, -1, width)
    return (
        out,
        gfeat,
        total[:, :width],
        total[:, width : 2 * width],
        total[:, 2 * width : 3 * width],
        total[:, 3 * width],
    )


def solution(mesh):
    return jax.shard_map(
        per_device,
        mesh=mesh,
        in_specs=(
            P(("row", "col"), None),
            P(),
            P(),
            P(),
            P(),
            P(("row", "col")),
            P(("row", "col")),
            P(("row", "col"), None, None),
            P(("row", "col")),
            P(("row", "col")),
            P(("row", "col"), None),
        ),
        out_specs=(P(("row", "col"), None), P(("row", "col"), None), P(), P(), P(), P()),
        check_vma=False,
    )
```

```python
import functools

import jax
import jax.numpy as jnp
from jax import lax
from jax.experimental import pallas as pl
from jax.experimental.pallas import tpu as pltpu
from jax.sharding import PartitionSpec as P

MESH = pl.DeviceIdType.MESH
F32 = jnp.float32
BF16 = jnp.bfloat16
EXTRA = 16
C0 = 0.7978845608028654
C1 = 0.044715


def gelu(v):
    return 0.5 * v * (1.0 + jnp.tanh(C0 * (v + C1 * (v * v * v))))


def gelu_slope(v):
    t = jnp.tanh(C0 * (v + C1 * (v * v * v)))
    return 0.5 * (1.0 + t) + 0.5 * v * (1.0 - t * t) * (C0 * (1.0 + 3.0 * C1 * (v * v)))


def dot(a, b):
    return jnp.dot(a, b, preferred_element_type=F32)


def dot_nt(a, b):
    return lax.dot_general(a, b, (((1,), (1,)), ((), ())), preferred_element_type=F32)


def dot_tn(a, b):
    return lax.dot_general(a, b, (((0,), (0,)), ((), ())), preferred_element_type=F32)


def kernel(
    rows,
    cols,
    feat,
    w_in,
    w_out,
    w_self,
    bias,
    out_deg,
    in_deg,
    cot,
    pick,
    count,
    tiles,
    out_ref,
    gfeat_ref,
    grads_ref,
    block,
    sib_block,
    staged,
    xc,
    xr,
    send_d,
    recv_d,
    send_r,
    recv_r,
    own_d,
    own_r,
    s_in,
    s_out,
    hs,
    ms_in,
    ms_out,
    zs,
    up,
    gz_ref,
    g_full,
    g_send,
    g_recv,
    gc_send,
    gc_recv,
    gz_send,
    gz_recv,
    g_all,
    tile_sem,
    blk_sem,
    xr_sem,
    xrs_sem,
    xcr_sem,
    xcl_sem,
    xcs_sem,
    d_sem,
    r_sem,
    gs_sem,
    gc_sem,
    gz_sem,
    az_sem,
    ac_sem,
    as_sem,
):
    chips = rows // 2
    nodes, width = feat.shape
    layers = w_in.shape[0]
    tile = staged.shape[1]
    sub = nodes // tile
    slots = staged.shape[0]
    per = slots // (rows * cols)
    row = lax.axis_index("row")
    c = lax.axis_index("col")
    k = lax.rem(row, 2)
    z = row // 2
    other = 1 - k
    sibling = (2 * z + other, c)

    def remote(src, dst, sems, index, device, parity=None):
        where = (index,) if parity is None else (parity, index)
        return pltpu.make_async_remote_copy(
            src_ref=src,
            dst_ref=dst,
            send_sem=sems.at[(0,) + where],
            recv_sem=sems.at[(1,) + where],
            device_id=device,
            device_id_type=MESH,
        )

    def at_chip(zz):
        return (2 * zz + k, c)

    def at_col(cc):
        return (row, cc)

    barrier = pltpu.get_barrier_semaphore()
    pl.semaphore_signal(barrier, inc=1, device_id=sibling, device_id_type=MESH)
    for off in range(1, chips):
        pl.semaphore_signal(
            barrier, inc=1, device_id=at_chip(lax.rem(z + off, chips)), device_id_type=MESH
        )
    for off in range(1, cols):
        pl.semaphore_signal(
            barrier, inc=1, device_id=at_col(lax.rem(c + off, cols)), device_id_type=MESH
        )

    strip = cols * per

    def tile_copy(rr):
        span = pl.ds(rr * strip, strip)
        return pltpu.make_async_copy(tiles.at[span], staged.at[span], tile_sem.at[rr])

    for kk in (other, k):
        for zz in range(chips):
            tile_copy(2 * zz + kk).start()

    for deg, scale in ((out_deg, s_out), (in_deg, s_in)):
        line = 1.0 / jnp.sqrt(deg[...].astype(F32))
        scale[...] = jnp.transpose(jnp.broadcast_to(line, (width, nodes)))
    hs[0] = feat[...]

    pl.semaphore_wait(barrier, chips + cols - 1)

    def build():
        for kk in (other, k):

            @pl.loop(0, chips)
            def _(zz):
                rr = 2 * zz + kk
                tile_copy(rr).wait()

                @pl.loop(0, cols)
                def _(cc):
                    first = (rr * cols + cc) * per
                    values = []
                    weights = []
                    for s in range(per):
                        values.append(staged[first + s].astype(F32))
                        live = first + s < count[0]
                        weights.append(jnp.where(live, pick[first + s], -1))
                    for spot in range(sub * sub):
                        total = jnp.zeros((tile, tile), F32)
                        for s in range(per):
                            factor = jnp.where(weights[s] == spot, 1.0, 0.0)
                            total = total + factor * values[s]
                        top = pl.multiple_of(cc * nodes + (spot // sub) * tile, tile)
                        left = pl.multiple_of(zz * nodes + (spot % sub) * tile, tile)
                        block[kk, pl.ds(top, tile), pl.ds(left, tile)] = total.astype(BF16)

            if kk is other:
                remote(block.at[other], sib_block, blk_sem, 0, sibling).start()

    def window(zz):
        return pl.ds(pl.multiple_of(zz * nodes, nodes), nodes)

    def exchange(stage, first, second_t, points=()):
        p = lax.rem(stage, 2)

        def visit(number):
            if points:
                points[number]()

        def xr_copy(off):
            mine = xr.at[p, k, :, window(c)]
            return remote(mine, mine, xr_sem, off, at_col(lax.rem(c + off, cols)), p)

        def xrs_copy(off, kk):
            view = xr.at[p, kk, :, window(lax.rem(c + cols - off, cols))]
            return remote(view, view, xrs_sem, off, sibling, p)

        def xc_view(kk, zz):
            return xc.at[p, kk, window(zz), :]

        def xcr_copy(dist, zz):
            return remote(xc_view(k, zz), xc_view(k, zz), xcr_sem, dist, at_chip(z + 1), p)

        def xcl_copy(dist, zz):
            return remote(xc_view(k, zz), xc_view(k, zz), xcl_sem, dist, at_chip(z - 1), p)

        def xcs_copy(kk, zz):
            return remote(xc_view(kk, zz), xc_view(kk, zz), xcs_sem, zz, sibling, p)

        def d_copy(off):
            target = at_col(lax.rem(c + off, cols))
            return remote(send_d.at[off], recv_d.at[p, off], d_sem, off, target, p)

        def r_copy(off):
            target = at_chip(lax.rem(z + off, chips))
            return remote(send_r.at[off], recv_r.at[p, off], r_sem, off, target, p)

        xr[p, k, :, window(c)] = second_t
        xc[p, k, window(z), :] = first
        for off in range(1, cols):
            xr_copy(off).start()
        xrs_copy(0, k).start()

        @pl.when(z + 1 < chips)
        def _():
            xcr_copy(1, z).start()

        @pl.when(z > 0)
        def _():
            xcl_copy(1, z).start()

        xcs_copy(k, z).start()

        @pl.when(stage == 0)
        def _():
            build()

        visit(0)

        def take_xr(off):
            source = lax.rem(c + cols - off, cols)
            view = xr.at[p, k, :, window(source)]
            remote(view, view, xr_sem, off, at_col(source), p).wait_recv()
            xrs_copy(off, k).start()

        def take_xc(dist):
            @pl.when(z - dist >= 0)
            def _():
                xcr_copy(dist, z - dist).wait_recv()

                @pl.when(z + 1 < chips)
                def _():
                    xcr_copy(dist + 1, z - dist).start()

                xcs_copy(k, z - dist).start()

            @pl.when(z + dist < chips)
            def _():
                xcl_copy(dist, z + dist).wait_recv()

                @pl.when(z > 0)
                def _():
                    xcl_copy(dist + 1, z + dist).start()

                xcs_copy(k, z + dist).start()

        for off in range(1, cols):
            take_xr(off)
            if off == 1:
                take_xc(1)
        for off in range(cols):
            xrs_copy(off, other).wait_recv()

        @pl.when(stage == 0)
        def _():
            remote(block.at[other], sib_block, blk_sem, 0, sibling).wait_recv()

        lanes = lax.broadcasted_iota(jnp.int32, (EXTRA, nodes), 1)
        groups = lax.broadcasted_iota(jnp.int32, (EXTRA, nodes), 0) // (EXTRA // sub)
        chooser = jnp.where(lanes == groups * tile, 1.0, 0.0).astype(BF16)

        @pl.loop(0, chips)
        def _(step):
            off = lax.rem(step + 1, chips)
            at = window(lax.rem(z + off, chips))
            piece = dot(xr[p, k], block[k, :, at]) + dot(xr[p, other], sib_block[:, at])

            @pl.when(off > 0)
            def _():
                means = []
                for part in range(sub):
                    mean = jnp.mean(piece[:, part * tile : (part + 1) * tile], axis=1, keepdims=True)
                    means.append(jnp.broadcast_to(mean, (width, tile)))
                mean = jnp.concatenate(means, axis=1).astype(BF16)
                send_r[off, pl.ds(0, width), :] = (piece - mean.astype(F32)).astype(BF16)
                send_r[off, pl.ds(width, EXTRA), :] = dot_nt(chooser, mean).astype(BF16)
                r_copy(off).start()

            @pl.when(off == 0)
            def _():
                own_r[...] = piece

        visit(1)

        for dist in range(2, chips):
            take_xc(dist)

        @pl.loop(0, chips)
        def _(zz):
            xcs_copy(other, zz).wait_recv()

        @pl.loop(0, cols)
        def _(step):
            off = lax.rem(step + 1, cols)
            at = window(lax.rem(c + off, cols))
            piece = dot(block[0, at, :], xc[p, 0]) + dot(block[1, at, :], xc[p, 1])

            @pl.when(off > 0)
            def _():
                lines = []
                for part in range(sub):
                    span = slice(part * tile, (part + 1) * tile)
                    mean = jnp.mean(piece[span], axis=0, keepdims=True).astype(BF16).astype(F32)
                    send_d[off, pl.ds(part * tile, tile), :] = (piece[span] - mean).astype(BF16)
                    lines.append(jnp.broadcast_to(mean, (EXTRA // sub, width)))
                send_d[off, pl.ds(nodes, EXTRA), :] = jnp.concatenate(lines, axis=0).astype(BF16)
                d_copy(off).start()

            @pl.when(off == 0)
            def _():
                own_d[...] = piece

        visit(2)

        def spread(lines):
            reach = EXTRA // sub
            return jnp.concatenate(
                [
                    jnp.broadcast_to(lines[part * reach : part * reach + 1], (tile, width))
                    for part in range(sub)
                ],
                axis=0,
            )

        lines = jnp.zeros((EXTRA, width), F32)
        for off in range(1, cols):
            d_copy(off).wait_recv()
            own_d[...] += recv_d[p, off, pl.ds(0, nodes), :].astype(F32)
            lines = lines + recv_d[p, off, pl.ds(nodes, EXTRA), :].astype(F32)
        direct = own_d[...] + spread(lines)
        visit(3)
        lines = jnp.zeros((EXTRA, width), F32)
        for off in range(1, chips):
            r_copy(off).wait_recv()
            own_r[...] += recv_r[p, off, pl.ds(0, width), :].astype(F32)
            lines = lines + recv_r[p, off, pl.ds(width, EXTRA), :].astype(F32)
        reverse = jnp.transpose(own_r[...]) + spread(lines)
        visit(4)

        for off in range(1, cols):
            xr_copy(off).wait_send()
            d_copy(off).wait_send()
        for off in range(cols):
            xrs_copy(off, k).wait_send()
        for off in range(1, chips):
            r_copy(off).wait_send()

        @pl.loop(0, chips)
        def _(zz):
            xcs_copy(k, zz).wait_send()

        for dist in range(1, chips):

            @pl.when(jnp.logical_and(z - dist + 1 >= 0, z + 1 < chips))
            def _():
                xcr_copy(dist, z - dist + 1).wait_send()

            @pl.when(jnp.logical_and(z + dist - 1 < chips, z > 0))
            def _():
                xcl_copy(dist, z + dist - 1).wait_send()

        return direct, reverse

    half = g_send.shape[0]
    depth = gz_send.shape[1]

    def reduction(layer, p):
        def to_sibling():
            return remote(g_send, g_recv.at[p], gs_sem, 0, sibling, p)

        def to_col(off):
            target = at_col(lax.rem(c + off, cols))
            return remote(gc_send.at[off], gc_recv.at[p, off], gc_sem, off, target, p)

        def to_chip(off):
            target = at_chip(lax.rem(z + off, chips))
            return remote(gz_send.at[off], gz_recv.at[p, off], gz_sem, off, target, p)

        def slot(kk, cc, zz, count):
            start = pl.multiple_of(((kk * cols + cc) * chips + zz) * depth, depth)
            return g_all.at[layer, pl.ds(start, count * depth), :]

        def spread_chip(off, zz):
            view = slot(k, c, zz, 1)
            return remote(view, view, az_sem, off, at_chip(lax.rem(z + off, chips)), p)

        def spread_col(off, cc):
            view = slot(k, cc, 0, chips)
            return remote(view, view, ac_sem, off, at_col(lax.rem(c + off, cols)), p)

        def spread_sibling(kk, cc):
            view = slot(kk, cc, 0, chips)
            return remote(view, view, as_sem, cc, sibling, p)

        def mine():
            return pl.ds(pl.multiple_of(k * half, half), half)

        def block_of(cc):
            return pl.ds(pl.multiple_of(k * half + cc * (chips * depth), depth), chips * depth)

        def share_of(zz):
            start = k * half + c * (chips * depth) + zz * depth
            return pl.ds(pl.multiple_of(start, depth), depth)

        def start():
            width = gz_ref.shape[1]
            grad = gz_ref[...]
            for at, left in enumerate((ms_in, ms_out, hs)):
                g_full[pl.ds(at * width, width), :] = dot_tn(left[layer], grad)
            line = jnp.sum(grad.astype(F32), axis=0, keepdims=True)
            g_full[pl.ds(3 * width, 8), :] = jnp.broadcast_to(line, (8, width))
            theirs = pl.ds(pl.multiple_of(other * half, half), half)
            g_send[...] = g_full[theirs, :].astype(BF16)
            to_sibling().start()

        def over_cols():
            to_sibling().wait_recv()
            g_full[mine(), :] += g_recv[p].astype(F32)
            for off in range(1, cols):
                gc_send[off] = g_full[block_of(lax.rem(c + off, cols)), :].astype(BF16)
                to_col(off).start()

        def over_chips():
            for off in range(1, cols):
                to_col(off).wait_recv()
                g_full[block_of(c), :] += gc_recv[p, off].astype(F32)
            for off in range(1, chips):
                gz_send[off] = g_full[share_of(lax.rem(z + off, chips)), :].astype(BF16)
                to_chip(off).start()

        def back_chips():
            for off in range(1, chips):
                to_chip(off).wait_recv()
                g_full[share_of(z), :] += gz_recv[p, off].astype(F32)
            at = pl.multiple_of(((k * cols + c) * chips + z) * depth, depth)
            g_all[layer, pl.ds(at, depth), :] = g_full[share_of(z), :].astype(BF16)
            for off in range(1, chips):
                spread_chip(off, z).start()

        def back_cols():
            for off in range(1, chips):
                spread_chip(off, lax.rem(z + chips - off, chips)).wait_recv()
            for off in range(1, cols):
                spread_col(off, c).start()
            spread_sibling(k, c).start()
            for off in range(1, cols):
                source = lax.rem(c + cols - off, cols)
                spread_col(off, source).wait_recv()
                spread_sibling(k, source).start()
            for off in range(cols):
                spread_sibling(other, lax.rem(c + off, cols)).wait_recv()
            to_sibling().wait_send()
            for off in range(1, cols):
                to_col(off).wait_send()
                spread_col(off, c).wait_send()
            for off in range(1, chips):
                to_chip(off).wait_send()
                spread_chip(off, z).wait_send()
            for off in range(cols):
                spread_sibling(k, lax.rem(c + off, cols)).wait_send()

        return start, over_cols, over_chips, back_chips, back_cols

    g_full[...] = jnp.zeros(g_full.shape, F32)

    @pl.loop(0, layers)
    def _(layer):
        hidden = hs[layer].astype(F32)
        first = (s_in[...] * hidden).astype(BF16)
        second_t = jnp.transpose(s_out[...] * hidden).astype(BF16)
        direct, reverse = exchange(layer, first, second_t)
        msg_in = (s_out[...] * direct).astype(BF16)
        msg_out = (s_in[...] * reverse).astype(BF16)
        ms_in[layer] = msg_in
        ms_out[layer] = msg_out
        preact = dot(msg_in, w_in[layer]) + dot(msg_out, w_out[layer])
        preact = preact + dot(hs[layer], w_self[layer]) + bias[pl.ds(layer, 1), :]
        zs[layer] = preact
        hs[layer + 1] = gelu(preact).astype(BF16)

    out_ref[...] = hs[layers]
    up[...] = cot[...].astype(F32)

    @pl.loop(0, layers)
    def _(step):
        layer = layers - 1 - step
        grad_z = (up[...] * gelu_slope(zs[layer])).astype(BF16)
        gz_ref[...] = grad_z
        back_in = jnp.transpose(s_out[...] * dot_nt(grad_z, w_in[layer])).astype(BF16)
        back_out = (s_in[...] * dot_nt(grad_z, w_out[layer])).astype(BF16)
        direct, reverse = exchange(
            layers + step, back_out, back_in, reduction(layer, lax.rem(layers + step, 2))
        )
        up[...] = (
            s_out[...] * direct + s_in[...] * reverse + dot_nt(gz_ref[...], w_self[layer])
        )

    grads_ref[...] = g_all[...]
    gfeat_ref[...] = up[...]
    remote(block.at[other], sib_block, blk_sem, 0, sibling).wait_send()


def per_device(
    features,
    weight_in,
    weight_out,
    weight_self,
    layer_bias,
    out_degree,
    in_degree,
    tile_values,
    tile_pick,
    tile_count,
    cotangent,
):
    rows = lax.axis_size("row")
    cols = lax.axis_size("col")
    nodes, width = features.shape
    layers = weight_in.shape[0]
    slots, tile, unused = tile_values.shape
    chips = rows // 2
    depth = -(-(3 * width + 8) // (rows * cols * 16)) * 16
    total = rows * cols * depth
    vmem = pl.BlockSpec(memory_space=pltpu.VMEM)
    smem = pl.BlockSpec(memory_space=pltpu.SMEM)
    sems = pltpu.SemaphoreType.DMA
    out, gfeat, grads = pl.pallas_call(
        functools.partial(kernel, rows, cols),
        out_shape=(
            jax.ShapeDtypeStruct((nodes, width), BF16),
            jax.ShapeDtypeStruct((nodes, width), F32),
            jax.ShapeDtypeStruct((layers, total, width), BF16),
        ),
        in_specs=[vmem] * 8 + [smem] * 2 + [pl.BlockSpec(memory_space=pl.ANY)],
        out_specs=(vmem, vmem, vmem),
        scratch_shapes=[
            pltpu.VMEM((2, cols * nodes, chips * nodes), BF16),
            pltpu.VMEM((cols * nodes, chips * nodes), BF16),
            pltpu.VMEM((slots, tile, tile), BF16),
            pltpu.VMEM((2, 2, chips * nodes, width), BF16),
            pltpu.VMEM((2, 2, width, cols * nodes), BF16),
            pltpu.VMEM((cols, nodes + EXTRA, width), BF16),
            pltpu.VMEM((2, cols, nodes + EXTRA, width), BF16),
            pltpu.VMEM((chips, width + EXTRA, nodes), BF16),
            pltpu.VMEM((2, chips, width + EXTRA, nodes), BF16),
            pltpu.VMEM((nodes, width), F32),
            pltpu.VMEM((width, nodes), F32),
            pltpu.VMEM((nodes, width), F32),
            pltpu.VMEM((nodes, width), F32),
            pltpu.VMEM((layers + 1, nodes, width), BF16),
            pltpu.VMEM((layers, nodes, width), BF16),
            pltpu.VMEM((layers, nodes, width), BF16),
            pltpu.VMEM((layers, nodes, width), F32),
            pltpu.VMEM((nodes, width), F32),
            pltpu.VMEM((nodes, width), BF16),
            pltpu.VMEM((total, width), F32),
            pltpu.VMEM((total // 2, width), BF16),
            pltpu.VMEM((2, total // 2, width), BF16),
            pltpu.VMEM((cols, chips * depth, width), BF16),
            pltpu.VMEM((2, cols, chips * depth, width), BF16),
            pltpu.VMEM((chips, depth, width), BF16),
            pltpu.VMEM((2, chips, depth, width), BF16),
            pltpu.VMEM((layers, total, width), BF16),
            sems((rows,)),
            sems((2, 1)),
            sems((2, 2, cols)),
            sems((2, 2, cols)),
            sems((2, 2, chips + 1)),
            sems((2, 2, chips + 1)),
            sems((2, 2, chips)),
            sems((2, 2, cols)),
            sems((2, 2, chips)),
            sems((2, 2, 1)),
            sems((2, 2, cols)),
            sems((2, 2, chips)),
            sems((2, 2, chips)),
            sems((2, 2, cols)),
            sems((2, 2, cols)),
        ],
        compiler_params=pltpu.CompilerParams(
            collective_id=0, has_side_effects=True, vmem_limit_bytes=63 * 1024 * 1024
        ),
    )(
        features,
        weight_in,
        weight_out,
        weight_self,
        layer_bias,
        out_degree.reshape(1, nodes),
        in_degree.reshape(1, nodes),
        cotangent,
        tile_pick,
        tile_count,
        tile_values,
    )
    grads = grads.astype(F32)
    return (
        out,
        gfeat,
        grads[:, :width],
        grads[:, width : 2 * width],
        grads[:, 2 * width : 3 * width],
        grads[:, 3 * width],
    )


def solution(mesh):
    return jax.shard_map(
        per_device,
        mesh=mesh,
        in_specs=(
            P(("row", "col"), None),
            P(),
            P(),
            P(),
            P(),
            P(("row", "col")),
            P(("row", "col")),
            P(("row", "col"), None, None),
            P(("row", "col")),
            P(("row", "col")),
            P(("row", "col"), None),
        ),
        out_specs=(P(("row", "col"), None), P(("row", "col"), None), P(), P(), P(), P()),
        check_vma=False,
    )
```

```python
import functools

import jax
import jax.numpy as jnp
from jax import lax
from jax.experimental import pallas as pl
from jax.experimental.pallas import tpu as pltpu
from jax.sharding import PartitionSpec as P

MESH = pl.DeviceIdType.MESH
F32 = jnp.float32
BF16 = jnp.bfloat16
EXTRA = 16
C0 = 0.7978845608028654
C1 = 0.044715


def gelu(v):
    return 0.5 * v * (1.0 + jnp.tanh(C0 * (v + C1 * (v * v * v))))


def gelu_slope(v):
    t = jnp.tanh(C0 * (v + C1 * (v * v * v)))
    return 0.5 * (1.0 + t) + 0.5 * v * (1.0 - t * t) * (C0 * (1.0 + 3.0 * C1 * (v * v)))


def dot(a, b):
    return jnp.dot(a, b, preferred_element_type=F32)


def dot_nt(a, b):
    return lax.dot_general(a, b, (((1,), (1,)), ((), ())), preferred_element_type=F32)


def dot_tn(a, b):
    return lax.dot_general(a, b, (((0,), (0,)), ((), ())), preferred_element_type=F32)


def kernel(
    rows,
    cols,
    feat,
    w_in,
    w_out,
    w_self,
    bias,
    out_deg,
    in_deg,
    cot,
    pick,
    count,
    tiles,
    out_ref,
    gfeat_ref,
    grads_ref,
    block,
    sib_block,
    staged,
    xc,
    xr,
    send_d,
    recv_d,
    send_r,
    recv_r,
    own_d,
    own_r,
    sums_d,
    sums_r,
    s_in,
    s_out,
    hs,
    ms_in,
    ms_out,
    zs,
    up,
    gz_ref,
    g_full,
    g_send,
    g_recv,
    gc_send,
    gc_recv,
    gz_send,
    gz_recv,
    g_all,
    tile_sem,
    blk_sem,
    xr_sem,
    xrs_sem,
    xcr_sem,
    xcl_sem,
    xcs_sem,
    d_sem,
    r_sem,
    gs_sem,
    gc_sem,
    gz_sem,
    az_sem,
    ac_sem,
    as_sem,
):
    chips = rows // 2
    nodes, width = feat.shape
    layers = w_in.shape[0]
    tile = staged.shape[1]
    sub = nodes // tile
    part_width = width // 2
    slots = staged.shape[0]
    per = slots // (rows * cols)
    row = lax.axis_index("row")
    c = lax.axis_index("col")
    k = lax.rem(row, 2)
    z = row // 2
    other = 1 - k
    sibling = (2 * z + other, c)

    def remote(src, dst, sems, index, device, parity=None):
        where = (index,) if parity is None else (parity, index)
        return pltpu.make_async_remote_copy(
            src_ref=src,
            dst_ref=dst,
            send_sem=sems.at[(0,) + where],
            recv_sem=sems.at[(1,) + where],
            device_id=device,
            device_id_type=MESH,
        )

    def at_chip(zz):
        return (2 * zz + k, c)

    def at_col(cc):
        return (row, cc)

    barrier = pltpu.get_barrier_semaphore()
    pl.semaphore_signal(barrier, inc=1, device_id=sibling, device_id_type=MESH)
    for off in range(1, chips):
        pl.semaphore_signal(
            barrier, inc=1, device_id=at_chip(lax.rem(z + off, chips)), device_id_type=MESH
        )
    for off in range(1, cols):
        pl.semaphore_signal(
            barrier, inc=1, device_id=at_col(lax.rem(c + off, cols)), device_id_type=MESH
        )

    strip = cols * per

    def tile_copy(rr):
        span = pl.ds(rr * strip, strip)
        return pltpu.make_async_copy(tiles.at[span], staged.at[span], tile_sem.at[rr])

    for kk in (other, k):
        for zz in range(chips):
            tile_copy(2 * zz + kk).start()

    for deg, scale in ((out_deg, s_out), (in_deg, s_in)):
        line = 1.0 / jnp.sqrt(deg[...].astype(F32))
        scale[...] = jnp.transpose(jnp.broadcast_to(line, (width, nodes)))
    hs[0] = feat[...]

    pl.semaphore_wait(barrier, chips + cols - 1)

    def build():
        for kk in (other, k):

            @pl.loop(0, chips)
            def _(zz):
                rr = 2 * zz + kk
                tile_copy(rr).wait()

                @pl.loop(0, cols)
                def _(cc):
                    first = (rr * cols + cc) * per
                    values = []
                    weights = []
                    for s in range(per):
                        values.append(staged[first + s].astype(F32))
                        live = first + s < count[0]
                        weights.append(jnp.where(live, pick[first + s], -1))
                    for spot in range(sub * sub):
                        total = jnp.zeros((tile, tile), F32)
                        for s in range(per):
                            factor = jnp.where(weights[s] == spot, 1.0, 0.0)
                            total = total + factor * values[s]
                        top = pl.multiple_of(cc * nodes + (spot // sub) * tile, tile)
                        left = pl.multiple_of(zz * nodes + (spot % sub) * tile, tile)
                        block[kk, pl.ds(top, tile), pl.ds(left, tile)] = total.astype(BF16)

            if kk is other:
                remote(block.at[other], sib_block, blk_sem, 0, sibling).start()

    def window(zz):
        return pl.ds(pl.multiple_of(zz * nodes, nodes), nodes)

    def exchange(stage, first, second_t, points=()):
        p = lax.rem(stage, 2)

        def visit(number):
            if points:
                points[number]()

        def xr_view(h, kk, cc):
            return xr.at[p, h, kk, :, window(cc)]

        def xr_copy(h, off):
            mine = xr_view(h, k, c)
            return remote(mine, mine, xr_sem, h * cols + off, at_col(lax.rem(c + off, cols)), p)

        def xrs_copy(h, off, kk):
            view = xr_view(h, kk, lax.rem(c + cols - off, cols))
            return remote(view, view, xrs_sem, h * cols + off, sibling, p)

        def xc_view(h, kk, zz):
            return xc.at[p, h, kk, window(zz), :]

        def xcr_copy(h, dist, zz):
            view = xc_view(h, k, zz)
            return remote(view, view, xcr_sem, h * (chips + 1) + dist, at_chip(z + 1), p)

        def xcl_copy(h, dist, zz):
            view = xc_view(h, k, zz)
            return remote(view, view, xcl_sem, h * (chips + 1) + dist, at_chip(z - 1), p)

        def xcs_copy(h, kk, zz):
            view = xc_view(h, kk, zz)
            return remote(view, view, xcs_sem, h * chips + zz, sibling, p)

        def d_copy(h, off):
            target = at_col(lax.rem(c + off, cols))
            return remote(send_d.at[h, off], recv_d.at[p, h, off], d_sem, h * cols + off, target, p)

        def r_copy(h, way, dest):
            target = at_chip(z + 1 if way == 0 else z - 1)
            landing = recv_r.at[p, h, way, dest]
            return remote(send_r.at[h, dest], landing, r_sem, (h * 2 + way) * chips + dest, target, p)

        for h in range(2):
            span = slice(h * part_width, (h + 1) * part_width)
            xr[p, h, k, :, window(c)] = second_t[span, :]
            xc[p, h, k, window(z), :] = first[:, span]
        for h in range(2):
            for off in range(1, cols):
                xr_copy(h, off).start()

            @pl.when(z + 1 < chips)
            def _():
                xcr_copy(h, 1, z).start()

            @pl.when(z > 0)
            def _():
                xcl_copy(h, 1, z).start()

            xrs_copy(h, 0, k).start()
            xcs_copy(h, k, z).start()

        @pl.when(stage == 0)
        def _():
            build()

        visit(0)

        def take_xr(h, off):
            source = lax.rem(c + cols - off, cols)
            view = xr_view(h, k, source)
            remote(view, view, xr_sem, h * cols + off, at_col(source), p).wait_recv()
            xrs_copy(h, off, k).start()

        def take_xc(h, dist):
            @pl.when(z - dist >= 0)
            def _():
                xcr_copy(h, dist, z - dist).wait_recv()

                @pl.when(z + 1 < chips)
                def _():
                    xcr_copy(h, dist + 1, z - dist).start()

                xcs_copy(h, k, z - dist).start()

            @pl.when(z + dist < chips)
            def _():
                xcl_copy(h, dist, z + dist).wait_recv()

                @pl.when(z > 0)
                def _():
                    xcl_copy(h, dist + 1, z + dist).start()

                xcs_copy(h, k, z + dist).start()

        reach = EXTRA // sub
        lanes = lax.broadcasted_iota(jnp.int32, (EXTRA, nodes), 1)
        lines = lax.broadcasted_iota(jnp.int32, (EXTRA, nodes), 0)
        chooser = jnp.where(lanes == (lines // reach) * tile, 1.0, 0.0).astype(BF16)
        spreader = jnp.where(lines == (lanes // tile) * reach, 1.0, 0.0).astype(BF16)

        def reverse_products(h):
            for off in range(cols):
                xrs_copy(h, off, other).wait_recv()
            if h == 0:

                @pl.when(stage == 0)
                def _():
                    remote(block.at[other], sib_block, blk_sem, 0, sibling).wait_recv()

            @pl.loop(0, chips)
            def _(dest):
                at = window(dest)
                own_r[h, dest] = dot(xr[p, h, k], block[k, :, at]) + dot(
                    xr[p, h, other], sib_block[:, at]
                )

        def r_send(h, way, dest, total):
            means = []
            for part in range(sub):
                mean = jnp.mean(total[:, part * tile : (part + 1) * tile], axis=1, keepdims=True)
                means.append(jnp.broadcast_to(mean, (part_width, tile)))
            mean = jnp.concatenate(means, axis=1).astype(BF16)
            send_r[h, dest, pl.ds(0, part_width), :] = (total - mean.astype(F32)).astype(BF16)
            send_r[h, dest, pl.ds(part_width, EXTRA), pl.ds(0, part_width)] = dot_nt(
                chooser, mean
            ).astype(BF16)
            r_copy(h, way, dest).start()

        def r_take(h, way, dest):
            r_copy(h, way, dest).wait_recv()
            mean = recv_r[p, h, way, dest, pl.ds(part_width, EXTRA), pl.ds(0, part_width)]
            rest = recv_r[p, h, way, dest, pl.ds(0, part_width), :].astype(F32)
            return rest + dot_tn(mean, spreader)

        def r_first(h):
            for dist in range(chips - 1, 0, -1):

                @pl.when(z == 0)
                def _():
                    r_send(h, 0, dist, own_r[h, dist])

                @pl.when(z == chips - 1)
                def _():
                    r_send(h, 1, chips - 1 - dist, own_r[h, chips - 1 - dist])

        def r_relay(h, dist):
            @pl.when(jnp.logical_and(z > 0, z + dist < chips))
            def _():
                r_send(h, 0, z + dist, own_r[h, z + dist] + r_take(h, 0, z + dist))

            @pl.when(jnp.logical_and(z < chips - 1, z - dist >= 0))
            def _():
                r_send(h, 1, z - dist, own_r[h, z - dist] + r_take(h, 1, z - dist))

        def direct_products(h):
            @pl.loop(0, chips)
            def _(zz):
                xcs_copy(h, other, zz).wait_recv()

            @pl.loop(0, cols)
            def _(step):
                off = lax.rem(step + 1, cols)
                at = window(lax.rem(c + off, cols))
                piece = dot(block[0, at, :], xc[p, h, 0]) + dot(block[1, at, :], xc[p, h, 1])

                @pl.when(off > 0)
                def _():
                    heads = []
                    for part in range(sub):
                        span = slice(part * tile, (part + 1) * tile)
                        mean = jnp.mean(piece[span], axis=0, keepdims=True).astype(BF16).astype(F32)
                        send_d[h, off, pl.ds(part * tile, tile), :] = (piece[span] - mean).astype(BF16)
                        heads.append(jnp.broadcast_to(mean, (reach, part_width)))
                    send_d[h, off, pl.ds(nodes, EXTRA), :] = jnp.concatenate(heads, axis=0).astype(BF16)
                    d_copy(h, off).start()

                @pl.when(off == 0)
                def _():
                    own_d[h] = piece

        def spread(lines):
            return jnp.concatenate(
                [
                    jnp.broadcast_to(lines[part * reach : part * reach + 1], (tile, part_width))
                    for part in range(sub)
                ],
                axis=0,
            )

        def direct_total(h):
            total = own_d[h]
            heads = jnp.zeros((EXTRA, part_width), F32)
            for off in range(1, cols):
                d_copy(h, off).wait_recv()
                total = total + recv_d[p, h, off, pl.ds(0, nodes), :].astype(F32)
                heads = heads + recv_d[p, h, off, pl.ds(nodes, EXTRA), :].astype(F32)
            sums_d[:, pl.ds(h * part_width, part_width)] = total + spread(heads)

        def reverse_total(h):
            @pl.when(z > 0)
            def _():
                own_r[h, z] += r_take(h, 0, z)

            @pl.when(z < chips - 1)
            def _():
                own_r[h, z] += r_take(h, 1, z)

            sums_r[:, pl.ds(h * part_width, part_width)] = jnp.transpose(own_r[h, z])

        for off in range(1, cols):
            take_xr(0, off)
            if off <= 2:
                take_xc(off - 1, 1)
        reverse_products(0)
        r_first(0)
        for dist in range(2, max(3, chips - 1)):
            take_xc(0, dist)
            take_xc(1, dist)
        visit(1)
        for off in range(1, cols):
            take_xr(1, off)
        reverse_products(1)
        r_first(1)
        for dist in range(chips - 2, 0, -1):
            r_relay(0, dist)
            if dist == chips - 2:
                take_xc(0, chips - 1)
                take_xc(1, chips - 1)
        direct_products(0)
        for dist in range(chips - 2, 0, -1):
            r_relay(1, dist)
        visit(2)
        direct_products(1)
        visit(3)
        for h in range(2):
            direct_total(h)
            reverse_total(h)
        visit(4)

        for h in range(2):
            for off in range(1, cols):
                xr_copy(h, off).wait_send()
                d_copy(h, off).wait_send()
            for off in range(cols):
                xrs_copy(h, off, k).wait_send()

            @pl.loop(0, chips)
            def _(zz):
                xcs_copy(h, k, zz).wait_send()

            for dist in range(1, chips):

                @pl.when(z + dist < chips)
                def _():
                    r_copy(h, 0, z + dist).wait_send()

                @pl.when(z - dist >= 0)
                def _():
                    r_copy(h, 1, z - dist).wait_send()

                @pl.when(jnp.logical_and(z - dist + 1 >= 0, z + 1 < chips))
                def _():
                    xcr_copy(h, dist, z - dist + 1).wait_send()

                @pl.when(jnp.logical_and(z + dist - 1 < chips, z > 0))
                def _():
                    xcl_copy(h, dist, z + dist - 1).wait_send()

        return sums_d[...], sums_r[...]

    half = g_send.shape[0]
    depth = gz_send.shape[1]

    def reduction(layer, p):
        def to_sibling():
            return remote(g_send, g_recv.at[p], gs_sem, 0, sibling, p)

        def to_col(off):
            target = at_col(lax.rem(c + off, cols))
            return remote(gc_send.at[off], gc_recv.at[p, off], gc_sem, off, target, p)

        def to_chip(off):
            target = at_chip(lax.rem(z + off, chips))
            return remote(gz_send.at[off], gz_recv.at[p, off], gz_sem, off, target, p)

        def slot(kk, cc, zz, count):
            start = pl.multiple_of(((kk * cols + cc) * chips + zz) * depth, depth)
            return g_all.at[layer, pl.ds(start, count * depth), :]

        def spread_chip(off, zz):
            view = slot(k, c, zz, 1)
            return remote(view, view, az_sem, off, at_chip(lax.rem(z + off, chips)), p)

        def spread_col(off, cc):
            view = slot(k, cc, 0, chips)
            return remote(view, view, ac_sem, off, at_col(lax.rem(c + off, cols)), p)

        def spread_sibling(kk, cc):
            view = slot(kk, cc, 0, chips)
            return remote(view, view, as_sem, cc, sibling, p)

        def mine():
            return pl.ds(pl.multiple_of(k * half, half), half)

        def block_of(cc):
            return pl.ds(pl.multiple_of(k * half + cc * (chips * depth), depth), chips * depth)

        def share_of(zz):
            start = k * half + c * (chips * depth) + zz * depth
            return pl.ds(pl.multiple_of(start, depth), depth)

        def start():
            width = gz_ref.shape[1]
            grad = gz_ref[...]
            for at, left in enumerate((ms_in, ms_out, hs)):
                g_full[pl.ds(at * width, width), :] = dot_tn(left[layer], grad)
            line = jnp.sum(grad.astype(F32), axis=0, keepdims=True)
            g_full[pl.ds(3 * width, 8), :] = jnp.broadcast_to(line, (8, width))
            theirs = pl.ds(pl.multiple_of(other * half, half), half)
            g_send[...] = g_full[theirs, :].astype(BF16)
            to_sibling().start()

        def over_cols():
            to_sibling().wait_recv()
            g_full[mine(), :] += g_recv[p].astype(F32)
            for off in range(1, cols):
                gc_send[off] = g_full[block_of(lax.rem(c + off, cols)), :].astype(BF16)
                to_col(off).start()

        def over_chips():
            for off in range(1, cols):
                to_col(off).wait_recv()
                g_full[block_of(c), :] += gc_recv[p, off].astype(F32)
            for off in range(1, chips):
                gz_send[off] = g_full[share_of(lax.rem(z + off, chips)), :].astype(BF16)
                to_chip(off).start()

        def back_chips():
            for off in range(1, chips):
                to_chip(off).wait_recv()
                g_full[share_of(z), :] += gz_recv[p, off].astype(F32)
            at = pl.multiple_of(((k * cols + c) * chips + z) * depth, depth)
            g_all[layer, pl.ds(at, depth), :] = g_full[share_of(z), :].astype(BF16)
            for off in range(1, chips):
                spread_chip(off, z).start()

        def back_cols():
            for off in range(1, chips):
                spread_chip(off, lax.rem(z + chips - off, chips)).wait_recv()
            for off in range(1, cols):
                spread_col(off, c).start()
            spread_sibling(k, c).start()
            for off in range(1, cols):
                source = lax.rem(c + cols - off, cols)
                spread_col(off, source).wait_recv()
                spread_sibling(k, source).start()
            for off in range(cols):
                spread_sibling(other, lax.rem(c + off, cols)).wait_recv()
            to_sibling().wait_send()
            for off in range(1, cols):
                to_col(off).wait_send()
                spread_col(off, c).wait_send()
            for off in range(1, chips):
                to_chip(off).wait_send()
                spread_chip(off, z).wait_send()
            for off in range(cols):
                spread_sibling(k, lax.rem(c + off, cols)).wait_send()

        return start, over_cols, over_chips, back_chips, back_cols

    g_full[...] = jnp.zeros(g_full.shape, F32)

    @pl.loop(0, layers)
    def _(layer):
        hidden = hs[layer].astype(F32)
        first = (s_in[...] * hidden).astype(BF16)
        second_t = jnp.transpose(s_out[...] * hidden).astype(BF16)
        direct, reverse = exchange(layer, first, second_t)
        msg_in = (s_out[...] * direct).astype(BF16)
        msg_out = (s_in[...] * reverse).astype(BF16)
        ms_in[layer] = msg_in
        ms_out[layer] = msg_out
        preact = dot(msg_in, w_in[layer]) + dot(msg_out, w_out[layer])
        preact = preact + dot(hs[layer], w_self[layer]) + bias[pl.ds(layer, 1), :]
        zs[layer] = preact
        hs[layer + 1] = gelu(preact).astype(BF16)

    out_ref[...] = hs[layers]
    up[...] = cot[...].astype(F32)

    @pl.loop(0, layers)
    def _(step):
        layer = layers - 1 - step
        grad_z = (up[...] * gelu_slope(zs[layer])).astype(BF16)
        gz_ref[...] = grad_z
        back_in = jnp.transpose(s_out[...] * dot_nt(grad_z, w_in[layer])).astype(BF16)
        back_out = (s_in[...] * dot_nt(grad_z, w_out[layer])).astype(BF16)
        direct, reverse = exchange(
            layers + step, back_out, back_in, reduction(layer, lax.rem(layers + step, 2))
        )
        up[...] = (
            s_out[...] * direct + s_in[...] * reverse + dot_nt(gz_ref[...], w_self[layer])
        )

    grads_ref[...] = g_all[...]
    gfeat_ref[...] = up[...]
    remote(block.at[other], sib_block, blk_sem, 0, sibling).wait_send()


def per_device(
    features,
    weight_in,
    weight_out,
    weight_self,
    layer_bias,
    out_degree,
    in_degree,
    tile_values,
    tile_pick,
    tile_count,
    cotangent,
):
    rows = lax.axis_size("row")
    cols = lax.axis_size("col")
    nodes, width = features.shape
    layers = weight_in.shape[0]
    slots, tile, unused = tile_values.shape
    chips = rows // 2
    part_width = width // 2
    depth = -(-(3 * width + 8) // (rows * cols * 16)) * 16
    total = rows * cols * depth
    vmem = pl.BlockSpec(memory_space=pltpu.VMEM)
    smem = pl.BlockSpec(memory_space=pltpu.SMEM)
    sems = pltpu.SemaphoreType.DMA
    out, gfeat, grads = pl.pallas_call(
        functools.partial(kernel, rows, cols),
        out_shape=(
            jax.ShapeDtypeStruct((nodes, width), BF16),
            jax.ShapeDtypeStruct((nodes, width), F32),
            jax.ShapeDtypeStruct((layers, total, width), BF16),
        ),
        in_specs=[vmem] * 8 + [smem] * 2 + [pl.BlockSpec(memory_space=pl.ANY)],
        out_specs=(vmem, vmem, vmem),
        scratch_shapes=[
            pltpu.VMEM((2, cols * nodes, chips * nodes), BF16),
            pltpu.VMEM((cols * nodes, chips * nodes), BF16),
            pltpu.VMEM((slots, tile, tile), BF16),
            pltpu.VMEM((2, 2, 2, chips * nodes, part_width), BF16),
            pltpu.VMEM((2, 2, 2, part_width, cols * nodes), BF16),
            pltpu.VMEM((2, cols, nodes + EXTRA, part_width), BF16),
            pltpu.VMEM((2, 2, cols, nodes + EXTRA, part_width), BF16),
            pltpu.VMEM((2, chips, part_width + EXTRA, nodes), BF16),
            pltpu.VMEM((2, 2, 2, chips, part_width + EXTRA, nodes), BF16),
            pltpu.VMEM((2, nodes, part_width), F32),
            pltpu.VMEM((2, chips, part_width, nodes), F32),
            pltpu.VMEM((nodes, width), F32),
            pltpu.VMEM((nodes, width), F32),
            pltpu.VMEM((nodes, width), F32),
            pltpu.VMEM((nodes, width), F32),
            pltpu.VMEM((layers + 1, nodes, width), BF16),
            pltpu.VMEM((layers, nodes, width), BF16),
            pltpu.VMEM((layers, nodes, width), BF16),
            pltpu.VMEM((layers, nodes, width), F32),
            pltpu.VMEM((nodes, width), F32),
            pltpu.VMEM((nodes, width), BF16),
            pltpu.VMEM((total, width), F32),
            pltpu.VMEM((total // 2, width), BF16),
            pltpu.VMEM((2, total // 2, width), BF16),
            pltpu.VMEM((cols, chips * depth, width), BF16),
            pltpu.VMEM((2, cols, chips * depth, width), BF16),
            pltpu.VMEM((chips, depth, width), BF16),
            pltpu.VMEM((2, chips, depth, width), BF16),
            pltpu.VMEM((layers, total, width), BF16),
            sems((rows,)),
            sems((2, 1)),
            sems((2, 2, 2 * cols)),
            sems((2, 2, 2 * cols)),
            sems((2, 2, 2 * (chips + 1))),
            sems((2, 2, 2 * (chips + 1))),
            sems((2, 2, 2 * chips)),
            sems((2, 2, 2 * cols)),
            sems((2, 2, 4 * chips)),
            sems((2, 2, 1)),
            sems((2, 2, cols)),
            sems((2, 2, chips)),
            sems((2, 2, chips)),
            sems((2, 2, cols)),
            sems((2, 2, cols)),
        ],
        compiler_params=pltpu.CompilerParams(
            collective_id=0, has_side_effects=True, vmem_limit_bytes=63 * 1024 * 1024
        ),
    )(
        features,
        weight_in,
        weight_out,
        weight_self,
        layer_bias,
        out_degree.reshape(1, nodes),
        in_degree.reshape(1, nodes),
        cotangent,
        tile_pick,
        tile_count,
        tile_values,
    )
    grads = grads.astype(F32)
    return (
        out,
        gfeat,
        grads[:, :width],
        grads[:, width : 2 * width],
        grads[:, 2 * width : 3 * width],
        grads[:, 3 * width],
    )


def solution(mesh):
    return jax.shard_map(
        per_device,
        mesh=mesh,
        in_specs=(
            P(("row", "col"), None),
            P(),
            P(),
            P(),
            P(),
            P(("row", "col")),
            P(("row", "col")),
            P(("row", "col"), None, None),
            P(("row", "col")),
            P(("row", "col")),
            P(("row", "col"), None),
        ),
        out_specs=(P(("row", "col"), None), P(("row", "col"), None), P(), P(), P(), P()),
        check_vma=False,
    )
```

```python
import functools

import jax
import jax.numpy as jnp
from jax import lax
from jax.experimental import pallas as pl
from jax.experimental.pallas import tpu as pltpu
from jax.sharding import PartitionSpec as P

MESH = pl.DeviceIdType.MESH
F32 = jnp.float32
BF16 = jnp.bfloat16
EXTRA = 16
C0 = 0.7978845608028654
C1 = 0.044715


def gelu(v):
    return 0.5 * v * (1.0 + jnp.tanh(C0 * (v + C1 * (v * v * v))))


def gelu_slope(v):
    t = jnp.tanh(C0 * (v + C1 * (v * v * v)))
    return 0.5 * (1.0 + t) + 0.5 * v * (1.0 - t * t) * (C0 * (1.0 + 3.0 * C1 * (v * v)))


def dot(a, b):
    return jnp.dot(a, b, preferred_element_type=F32)


def dot_nt(a, b):
    return lax.dot_general(a, b, (((1,), (1,)), ((), ())), preferred_element_type=F32)


def dot_tn(a, b):
    return lax.dot_general(a, b, (((0,), (0,)), ((), ())), preferred_element_type=F32)


def kernel(
    rows,
    cols,
    feat,
    w_in,
    w_out,
    w_self,
    bias,
    out_deg,
    in_deg,
    cot,
    pick,
    count,
    tiles,
    out_ref,
    gfeat_ref,
    grads_ref,
    block,
    sib_block,
    staged,
    xc,
    xr,
    send_d,
    recv_d,
    send_r,
    recv_r,
    own_d,
    own_r,
    sums_d,
    sums_r,
    s_in,
    s_out,
    hs,
    ms_in,
    ms_out,
    zs,
    up,
    gz_ref,
    g_full,
    g_send,
    g_recv,
    gc_send,
    gc_recv,
    gz_send,
    gz_recv,
    g_all,
    tile_sem,
    blk_sem,
    xr_sem,
    xrs_sem,
    xcr_sem,
    xcl_sem,
    xcs_sem,
    d_sem,
    r_sem,
    gs_sem,
    gc_sem,
    gz_sem,
    az_sem,
    ac_sem,
    as_sem,
):
    chips = rows // 2
    nodes, width = feat.shape
    layers = w_in.shape[0]
    tile = staged.shape[1]
    sub = nodes // tile
    part_width = width // 2
    slots = staged.shape[0]
    per = slots // (rows * cols)
    row = lax.axis_index("row")
    c = lax.axis_index("col")
    k = lax.rem(row, 2)
    z = row // 2
    other = 1 - k
    sibling = (2 * z + other, c)

    def remote(src, dst, sems, index, device, parity=None):
        where = (index,) if parity is None else (parity, index)
        return pltpu.make_async_remote_copy(
            src_ref=src,
            dst_ref=dst,
            send_sem=sems.at[(0,) + where],
            recv_sem=sems.at[(1,) + where],
            device_id=device,
            device_id_type=MESH,
        )

    def at_chip(zz):
        return (2 * zz + k, c)

    def at_col(cc):
        return (row, cc)

    barrier = pltpu.get_barrier_semaphore()
    pl.semaphore_signal(barrier, inc=1, device_id=sibling, device_id_type=MESH)
    for off in range(1, chips):
        pl.semaphore_signal(
            barrier, inc=1, device_id=at_chip(lax.rem(z + off, chips)), device_id_type=MESH
        )
    for off in range(1, cols):
        pl.semaphore_signal(
            barrier, inc=1, device_id=at_col(lax.rem(c + off, cols)), device_id_type=MESH
        )

    strip = cols * per

    def tile_copy(rr):
        span = pl.ds(rr * strip, strip)
        return pltpu.make_async_copy(tiles.at[span], staged.at[span], tile_sem.at[rr])

    for kk in (other, k):
        for zz in range(chips):
            tile_copy(2 * zz + kk).start()

    for deg, scale in ((out_deg, s_out), (in_deg, s_in)):
        line = 1.0 / jnp.sqrt(deg[...].astype(F32))
        scale[...] = jnp.transpose(jnp.broadcast_to(line, (width, nodes)))
    hs[0] = feat[...]

    pl.semaphore_wait(barrier, chips + cols - 1)

    def build():
        for kk in (other, k):

            @pl.loop(0, chips)
            def _(zz):
                rr = 2 * zz + kk
                tile_copy(rr).wait()

                @pl.loop(0, cols)
                def _(cc):
                    first = (rr * cols + cc) * per
                    values = []
                    weights = []
                    for s in range(per):
                        values.append(staged[first + s].astype(F32))
                        live = first + s < count[0]
                        weights.append(jnp.where(live, pick[first + s], -1))
                    for spot in range(sub * sub):
                        total = jnp.zeros((tile, tile), F32)
                        for s in range(per):
                            factor = jnp.where(weights[s] == spot, 1.0, 0.0)
                            total = total + factor * values[s]
                        top = pl.multiple_of(cc * nodes + (spot // sub) * tile, tile)
                        left = pl.multiple_of(zz * nodes + (spot % sub) * tile, tile)
                        block[kk, pl.ds(top, tile), pl.ds(left, tile)] = total.astype(BF16)

            if kk is other:
                remote(block.at[other], sib_block, blk_sem, 0, sibling).start()

    def window(zz):
        return pl.ds(pl.multiple_of(zz * nodes, nodes), nodes)

    def exchange(stage, first, second_t, points=(), centred=True):
        p = lax.rem(stage, 2)

        def visit(number):
            if points:
                points[number]()

        def xr_view(h, kk, cc):
            return xr.at[p, h, kk, :, window(cc)]

        def xr_copy(h, off):
            mine = xr_view(h, k, c)
            return remote(mine, mine, xr_sem, h * cols + off, at_col(lax.rem(c + off, cols)), p)

        def xrs_copy(h, off, kk):
            view = xr_view(h, kk, lax.rem(c + cols - off, cols))
            return remote(view, view, xrs_sem, h * cols + off, sibling, p)

        def xc_view(h, kk, zz):
            return xc.at[p, h, kk, window(zz), :]

        def xcr_copy(h, dist, zz):
            view = xc_view(h, k, zz)
            return remote(view, view, xcr_sem, h * (chips + 1) + dist, at_chip(z + 1), p)

        def xcl_copy(h, dist, zz):
            view = xc_view(h, k, zz)
            return remote(view, view, xcl_sem, h * (chips + 1) + dist, at_chip(z - 1), p)

        def xcs_copy(h, kk, zz):
            view = xc_view(h, kk, zz)
            return remote(view, view, xcs_sem, h * chips + zz, sibling, p)

        def d_copy(h, off):
            target = at_col(lax.rem(c + off, cols))
            span = pl.ds(0, nodes + (EXTRA if centred else 0))
            landing = recv_d.at[p, h, off, span]
            return remote(send_d.at[h, off, span], landing, d_sem, h * cols + off, target, p)

        def r_copy(h, way, dest):
            target = at_chip(z + 1 if way == 0 else z - 1)
            span = pl.ds(0, part_width + (EXTRA if centred else 0))
            landing = recv_r.at[p, h, way, dest, span]
            return remote(send_r.at[h, dest, span], landing, r_sem, (h * 2 + way) * chips + dest, target, p)

        for h in range(2):
            span = slice(h * part_width, (h + 1) * part_width)
            xr[p, h, k, :, window(c)] = second_t[span, :]
            xc[p, h, k, window(z), :] = first[:, span]
        for h in range(2):
            for off in range(1, cols):
                xr_copy(h, off).start()

            @pl.when(z + 1 < chips)
            def _():
                xcr_copy(h, 1, z).start()

            @pl.when(z > 0)
            def _():
                xcl_copy(h, 1, z).start()

            xrs_copy(h, 0, k).start()
            xcs_copy(h, k, z).start()

        @pl.when(stage == 0)
        def _():
            build()

        visit(0)

        def take_xr(h, off):
            source = lax.rem(c + cols - off, cols)
            view = xr_view(h, k, source)
            remote(view, view, xr_sem, h * cols + off, at_col(source), p).wait_recv()
            xrs_copy(h, off, k).start()

        def take_xc(h, dist):
            @pl.when(z - dist >= 0)
            def _():
                xcr_copy(h, dist, z - dist).wait_recv()

                @pl.when(z + 1 < chips)
                def _():
                    xcr_copy(h, dist + 1, z - dist).start()

                xcs_copy(h, k, z - dist).start()

            @pl.when(z + dist < chips)
            def _():
                xcl_copy(h, dist, z + dist).wait_recv()

                @pl.when(z > 0)
                def _():
                    xcl_copy(h, dist + 1, z + dist).start()

                xcs_copy(h, k, z + dist).start()

        reach = EXTRA // sub
        lanes = lax.broadcasted_iota(jnp.int32, (EXTRA, nodes), 1)
        lines = lax.broadcasted_iota(jnp.int32, (EXTRA, nodes), 0)
        chooser = jnp.where(lanes == (lines // reach) * tile, 1.0, 0.0).astype(BF16)
        spreader = jnp.where(lines == (lanes // tile) * reach, 1.0, 0.0).astype(BF16)

        def reverse_products(h):
            for off in range(cols):
                xrs_copy(h, off, other).wait_recv()
            if h == 0:

                @pl.when(stage == 0)
                def _():
                    remote(block.at[other], sib_block, blk_sem, 0, sibling).wait_recv()

            @pl.loop(0, chips)
            def _(dest):
                at = window(dest)
                own_r[h, dest] = dot(xr[p, h, k], block[k, :, at]) + dot(
                    xr[p, h, other], sib_block[:, at]
                )

        def r_send(h, way, dest, total):
            if not centred:
                send_r[h, dest, pl.ds(0, part_width), :] = total.astype(BF16)
                r_copy(h, way, dest).start()
                return
            means = []
            for part in range(sub):
                mean = jnp.mean(total[:, part * tile : (part + 1) * tile], axis=1, keepdims=True)
                means.append(jnp.broadcast_to(mean, (part_width, tile)))
            mean = jnp.concatenate(means, axis=1).astype(BF16)
            send_r[h, dest, pl.ds(0, part_width), :] = (total - mean.astype(F32)).astype(BF16)
            send_r[h, dest, pl.ds(part_width, EXTRA), pl.ds(0, part_width)] = dot_nt(
                chooser, mean
            ).astype(BF16)
            r_copy(h, way, dest).start()

        def r_take(h, way, dest):
            r_copy(h, way, dest).wait_recv()
            rest = recv_r[p, h, way, dest, pl.ds(0, part_width), :].astype(F32)
            if not centred:
                return rest
            mean = recv_r[p, h, way, dest, pl.ds(part_width, EXTRA), pl.ds(0, part_width)]
            return rest + dot_tn(mean, spreader)

        def r_first(h):
            for dist in range(chips - 1, 0, -1):

                @pl.when(z == 0)
                def _():
                    r_send(h, 0, dist, own_r[h, dist])

                @pl.when(z == chips - 1)
                def _():
                    r_send(h, 1, chips - 1 - dist, own_r[h, chips - 1 - dist])

        def r_relay(h, dist):
            @pl.when(jnp.logical_and(z > 0, z + dist < chips))
            def _():
                r_send(h, 0, z + dist, own_r[h, z + dist] + r_take(h, 0, z + dist))

            @pl.when(jnp.logical_and(z < chips - 1, z - dist >= 0))
            def _():
                r_send(h, 1, z - dist, own_r[h, z - dist] + r_take(h, 1, z - dist))

        def direct_products(h):
            @pl.loop(0, chips)
            def _(zz):
                xcs_copy(h, other, zz).wait_recv()

            @pl.loop(0, cols)
            def _(step):
                off = lax.rem(step + 1, cols)
                at = window(lax.rem(c + off, cols))
                piece = dot(block[0, at, :], xc[p, h, 0]) + dot(block[1, at, :], xc[p, h, 1])

                @pl.when(off > 0)
                def _():
                    if not centred:
                        send_d[h, off, pl.ds(0, nodes), :] = piece.astype(BF16)
                        d_copy(h, off).start()
                        return
                    heads = []
                    for part in range(sub):
                        span = slice(part * tile, (part + 1) * tile)
                        mean = jnp.mean(piece[span], axis=0, keepdims=True).astype(BF16).astype(F32)
                        send_d[h, off, pl.ds(part * tile, tile), :] = (piece[span] - mean).astype(BF16)
                        heads.append(jnp.broadcast_to(mean, (reach, part_width)))
                    send_d[h, off, pl.ds(nodes, EXTRA), :] = jnp.concatenate(heads, axis=0).astype(BF16)
                    d_copy(h, off).start()

                @pl.when(off == 0)
                def _():
                    own_d[h] = piece

        def spread(lines):
            return jnp.concatenate(
                [
                    jnp.broadcast_to(lines[part * reach : part * reach + 1], (tile, part_width))
                    for part in range(sub)
                ],
                axis=0,
            )

        def direct_total(h):
            total = own_d[h]
            heads = jnp.zeros((EXTRA, part_width), F32)
            for off in range(1, cols):
                d_copy(h, off).wait_recv()
                total = total + recv_d[p, h, off, pl.ds(0, nodes), :].astype(F32)
                if centred:
                    heads = heads + recv_d[p, h, off, pl.ds(nodes, EXTRA), :].astype(F32)
            if centred:
                total = total + spread(heads)
            sums_d[:, pl.ds(h * part_width, part_width)] = total

        def reverse_total(h):
            @pl.when(z > 0)
            def _():
                own_r[h, z] += r_take(h, 0, z)

            @pl.when(z < chips - 1)
            def _():
                own_r[h, z] += r_take(h, 1, z)

            sums_r[:, pl.ds(h * part_width, part_width)] = jnp.transpose(own_r[h, z])

        for off in range(1, cols):
            take_xr(0, off)
            if off <= 2:
                take_xc(off - 1, 1)
        reverse_products(0)
        r_first(0)
        for dist in range(2, max(3, chips - 1)):
            take_xc(0, dist)
            take_xc(1, dist)
        visit(1)
        for off in range(1, cols):
            take_xr(1, off)
        reverse_products(1)
        r_first(1)
        visit(2)
        take_xc(0, chips - 1)
        take_xc(1, chips - 1)
        direct_products(0)
        for dist in range(chips - 2, 0, -1):
            r_relay(0, dist)
        visit(3)
        direct_products(1)
        for dist in range(chips - 2, 0, -1):
            r_relay(1, dist)
        visit(4)
        direct_total(0)
        reverse_total(0)
        direct_total(1)
        visit(5)
        reverse_total(1)
        visit(6)

        for h in range(2):
            for off in range(1, cols):
                xr_copy(h, off).wait_send()
                d_copy(h, off).wait_send()
            for off in range(cols):
                xrs_copy(h, off, k).wait_send()

            @pl.loop(0, chips)
            def _(zz):
                xcs_copy(h, k, zz).wait_send()

            for dist in range(1, chips):

                @pl.when(z + dist < chips)
                def _():
                    r_copy(h, 0, z + dist).wait_send()

                @pl.when(z - dist >= 0)
                def _():
                    r_copy(h, 1, z - dist).wait_send()

                @pl.when(jnp.logical_and(z - dist + 1 >= 0, z + 1 < chips))
                def _():
                    xcr_copy(h, dist, z - dist + 1).wait_send()

                @pl.when(jnp.logical_and(z + dist - 1 < chips, z > 0))
                def _():
                    xcl_copy(h, dist, z + dist - 1).wait_send()

        return sums_d[...], sums_r[...]

    half = g_send.shape[0]
    depth = gz_send.shape[1]

    def reduction(layer, p):
        def to_sibling():
            return remote(g_send, g_recv.at[p], gs_sem, 0, sibling, p)

        def to_col(off):
            target = at_col(lax.rem(c + off, cols))
            return remote(gc_send.at[off], gc_recv.at[p, off], gc_sem, off, target, p)

        def to_chip(off):
            target = at_chip(lax.rem(z + off, chips))
            return remote(gz_send.at[off], gz_recv.at[p, off], gz_sem, off, target, p)

        def slot(kk, cc, zz, count):
            start = pl.multiple_of(((kk * cols + cc) * chips + zz) * depth, depth)
            return g_all.at[layer, pl.ds(start, count * depth), :]

        def spread_chip(off, zz):
            view = slot(k, c, zz, 1)
            return remote(view, view, az_sem, off, at_chip(lax.rem(z + off, chips)), p)

        def spread_col(off, cc):
            view = slot(k, cc, 0, chips)
            return remote(view, view, ac_sem, off, at_col(lax.rem(c + off, cols)), p)

        def spread_sibling(kk, cc):
            view = slot(kk, cc, 0, chips)
            return remote(view, view, as_sem, cc, sibling, p)

        def mine():
            return pl.ds(pl.multiple_of(k * half, half), half)

        def block_of(cc):
            return pl.ds(pl.multiple_of(k * half + cc * (chips * depth), depth), chips * depth)

        def share_of(zz):
            start = k * half + c * (chips * depth) + zz * depth
            return pl.ds(pl.multiple_of(start, depth), depth)

        def start():
            width = gz_ref.shape[1]
            grad = gz_ref[...]
            for at, left in enumerate((ms_in, ms_out, hs)):
                g_full[pl.ds(at * width, width), :] = dot_tn(left[layer], grad)
            line = jnp.sum(grad.astype(F32), axis=0, keepdims=True)
            g_full[pl.ds(3 * width, 8), :] = jnp.broadcast_to(line, (8, width))
            theirs = pl.ds(pl.multiple_of(other * half, half), half)
            g_send[...] = g_full[theirs, :].astype(BF16)
            to_sibling().start()

        def over_cols():
            to_sibling().wait_recv()
            g_full[mine(), :] += g_recv[p].astype(F32)
            for off in range(1, cols):
                gc_send[off] = g_full[block_of(lax.rem(c + off, cols)), :].astype(BF16)
                to_col(off).start()

        def over_chips():
            for off in range(1, cols):
                to_col(off).wait_recv()
                g_full[block_of(c), :] += gc_recv[p, off].astype(F32)
            for off in range(1, chips):
                gz_send[off] = g_full[share_of(lax.rem(z + off, chips)), :].astype(BF16)
                to_chip(off).start()

        def back_chips():
            for off in range(1, chips):
                to_chip(off).wait_recv()
                g_full[share_of(z), :] += gz_recv[p, off].astype(F32)
            at = pl.multiple_of(((k * cols + c) * chips + z) * depth, depth)
            g_all[layer, pl.ds(at, depth), :] = g_full[share_of(z), :].astype(BF16)
            for off in range(1, chips):
                spread_chip(off, z).start()

        def back_cols():
            for off in range(1, chips):
                spread_chip(off, lax.rem(z + chips - off, chips)).wait_recv()
            for off in range(1, cols):
                spread_col(off, c).start()
            spread_sibling(k, c).start()

        def pass_on():
            for off in range(1, cols):
                source = lax.rem(c + cols - off, cols)
                spread_col(off, source).wait_recv()
                spread_sibling(k, source).start()

        def finish():
            for off in range(cols):
                spread_sibling(other, lax.rem(c + off, cols)).wait_recv()
            to_sibling().wait_send()
            for off in range(1, cols):
                to_col(off).wait_send()
                spread_col(off, c).wait_send()
            for off in range(1, chips):
                to_chip(off).wait_send()
                spread_chip(off, z).wait_send()
            for off in range(cols):
                spread_sibling(k, lax.rem(c + off, cols)).wait_send()

        return start, over_cols, over_chips, back_chips, back_cols, pass_on, finish

    g_full[...] = jnp.zeros(g_full.shape, F32)

    @pl.loop(0, layers)
    def _(layer):
        hidden = hs[layer].astype(F32)
        first = (s_in[...] * hidden).astype(BF16)
        second_t = jnp.transpose(s_out[...] * hidden).astype(BF16)
        direct, reverse = exchange(layer, first, second_t)
        msg_in = (s_out[...] * direct).astype(BF16)
        msg_out = (s_in[...] * reverse).astype(BF16)
        ms_in[layer] = msg_in
        ms_out[layer] = msg_out
        preact = dot(msg_in, w_in[layer]) + dot(msg_out, w_out[layer])
        preact = preact + dot(hs[layer], w_self[layer]) + bias[pl.ds(layer, 1), :]
        zs[layer] = preact
        hs[layer + 1] = gelu(preact).astype(BF16)

    out_ref[...] = hs[layers]
    up[...] = cot[...].astype(F32)

    @pl.loop(0, layers)
    def _(step):
        layer = layers - 1 - step
        grad_z = (up[...] * gelu_slope(zs[layer])).astype(BF16)
        gz_ref[...] = grad_z
        back_in = jnp.transpose(s_out[...] * dot_nt(grad_z, w_in[layer])).astype(BF16)
        back_out = (s_in[...] * dot_nt(grad_z, w_out[layer])).astype(BF16)
        phases = reduction(layer, lax.rem(layers + step, 2))
        direct, reverse = exchange(layers + step, back_out, back_in, phases, centred=False)
        up[...] = (
            s_out[...] * direct + s_in[...] * reverse + dot_nt(gz_ref[...], w_self[layer])
        )

    grads_ref[...] = g_all[...]
    gfeat_ref[...] = up[...]
    remote(block.at[other], sib_block, blk_sem, 0, sibling).wait_send()


def per_device(
    features,
    weight_in,
    weight_out,
    weight_self,
    layer_bias,
    out_degree,
    in_degree,
    tile_values,
    tile_pick,
    tile_count,
    cotangent,
):
    rows = lax.axis_size("row")
    cols = lax.axis_size("col")
    nodes, width = features.shape
    layers = weight_in.shape[0]
    slots, tile, unused = tile_values.shape
    chips = rows // 2
    part_width = width // 2
    depth = -(-(3 * width + 8) // (rows * cols * 16)) * 16
    total = rows * cols * depth
    vmem = pl.BlockSpec(memory_space=pltpu.VMEM)
    smem = pl.BlockSpec(memory_space=pltpu.SMEM)
    sems = pltpu.SemaphoreType.DMA
    out, gfeat, grads = pl.pallas_call(
        functools.partial(kernel, rows, cols),
        out_shape=(
            jax.ShapeDtypeStruct((nodes, width), BF16),
            jax.ShapeDtypeStruct((nodes, width), F32),
            jax.ShapeDtypeStruct((layers, total, width), BF16),
        ),
        in_specs=[vmem] * 8 + [smem] * 2 + [pl.BlockSpec(memory_space=pl.ANY)],
        out_specs=(vmem, vmem, vmem),
        scratch_shapes=[
            pltpu.VMEM((2, cols * nodes, chips * nodes), BF16),
            pltpu.VMEM((cols * nodes, chips * nodes), BF16),
            pltpu.VMEM((slots, tile, tile), BF16),
            pltpu.VMEM((2, 2, 2, chips * nodes, part_width), BF16),
            pltpu.VMEM((2, 2, 2, part_width, cols * nodes), BF16),
            pltpu.VMEM((2, cols, nodes + EXTRA, part_width), BF16),
            pltpu.VMEM((2, 2, cols, nodes + EXTRA, part_width), BF16),
            pltpu.VMEM((2, chips, part_width + EXTRA, nodes), BF16),
            pltpu.VMEM((2, 2, 2, chips, part_width + EXTRA, nodes), BF16),
            pltpu.VMEM((2, nodes, part_width), F32),
            pltpu.VMEM((2, chips, part_width, nodes), F32),
            pltpu.VMEM((nodes, width), F32),
            pltpu.VMEM((nodes, width), F32),
            pltpu.VMEM((nodes, width), F32),
            pltpu.VMEM((nodes, width), F32),
            pltpu.VMEM((layers + 1, nodes, width), BF16),
            pltpu.VMEM((layers, nodes, width), BF16),
            pltpu.VMEM((layers, nodes, width), BF16),
            pltpu.VMEM((layers, nodes, width), F32),
            pltpu.VMEM((nodes, width), F32),
            pltpu.VMEM((nodes, width), BF16),
            pltpu.VMEM((total, width), F32),
            pltpu.VMEM((total // 2, width), BF16),
            pltpu.VMEM((2, total // 2, width), BF16),
            pltpu.VMEM((cols, chips * depth, width), BF16),
            pltpu.VMEM((2, cols, chips * depth, width), BF16),
            pltpu.VMEM((chips, depth, width), BF16),
            pltpu.VMEM((2, chips, depth, width), BF16),
            pltpu.VMEM((layers, total, width), BF16),
            sems((rows,)),
            sems((2, 1)),
            sems((2, 2, 2 * cols)),
            sems((2, 2, 2 * cols)),
            sems((2, 2, 2 * (chips + 1))),
            sems((2, 2, 2 * (chips + 1))),
            sems((2, 2, 2 * chips)),
            sems((2, 2, 2 * cols)),
            sems((2, 2, 4 * chips)),
            sems((2, 2, 1)),
            sems((2, 2, cols)),
            sems((2, 2, chips)),
            sems((2, 2, chips)),
            sems((2, 2, cols)),
            sems((2, 2, cols)),
        ],
        compiler_params=pltpu.CompilerParams(
            collective_id=0, has_side_effects=True, vmem_limit_bytes=63 * 1024 * 1024
        ),
    )(
        features,
        weight_in,
        weight_out,
        weight_self,
        layer_bias,
        out_degree.reshape(1, nodes),
        in_degree.reshape(1, nodes),
        cotangent,
        tile_pick,
        tile_count,
        tile_values,
    )
    grads = grads.astype(F32)
    return (
        out,
        gfeat,
        grads[:, :width],
        grads[:, width : 2 * width],
        grads[:, 2 * width : 3 * width],
        grads[:, 3 * width],
    )


def solution(mesh):
    return jax.shard_map(
        per_device,
        mesh=mesh,
        in_specs=(
            P(("row", "col"), None),
            P(),
            P(),
            P(),
            P(),
            P(("row", "col")),
            P(("row", "col")),
            P(("row", "col"), None, None),
            P(("row", "col")),
            P(("row", "col")),
            P(("row", "col"), None),
        ),
        out_specs=(P(("row", "col"), None), P(("row", "col"), None), P(), P(), P(), P()),
        check_vma=False,
    )
```
